256 devices in a mesh: ctx: 64 (over z, y_lo, x), head: 4 (over y_hi, core).
Axes of the slice: x: 4, y: 4 (y_hi: 2, y_lo: 2; y = y_hi * 2 + y_lo), z: 8, core: 2. Of those that a mesh axis runs over, the one named last changes fastest.
Arguments:
- queries: bfloat16 [8192, 1024], P('ctx', 'head'), may hold values from -27 to 27
- keys: bfloat16 [8192, 128], P('ctx'), may hold values from -4 to 4
- values: bfloat16 [8192, 128], P('ctx'), may hold values from -6 to 6
- dout: bfloat16 [8192, 1024], P('ctx', 'head'), may hold values from -6 to 6
- positions: int32 [8192], P('ctx'), may hold values from 0 to 8191, as said below
- doc_ids: int32 [8192], P('ctx'), may hold values from 0 to 127, as said below
- w_query: bfloat16 [1024, 16384], P('head'), may hold values from -0.1875 to 0.1875
- w_kv: bfloat16 [256, 16384], P(None, 'head'), may hold values from -0.375 to 0.375
Outputs:
- grad_input: bfloat16 [8192, 16384], P('ctx', 'head')
The draws below stay inside these ranges and needn't reach their ends.
Inputs may be any that keep to these rules, and one draw needn't show every extreme that they name: Stored rows come in aligned runs of 64 rows that hold 64 consecutive positions in order, starting at a multiple of 64; every position of the sequence is stored once. `doc_ids`: A document is a set of consecutive positions that begins at a multiple of 64; its id is its first position divided by 64. The first and the last run of 64 positions each begin a document.
All inputs are finite; a program needn't handle non-finite values.
Results may differ from the reference program's by a relative error of at most 0.019.
Values may be sent and summed in bfloat16 or wider, within the bound.
A program may use at most 128 MiB of HBM per device.

```python
import math
import jax
import jax.numpy as jnp
from jax import lax

D = 16384
HD = 128
QH = 8
ALIGN = 64
SEQ = 8192


def layout_tables(key):
    block_count = SEQ // ALIGN
    block_order = jax.random.permutation(jax.random.fold_in(key, 101), block_count).astype(jnp.int32)
    block_index = jnp.arange(block_count, dtype=jnp.int32)
    starts_flag = jax.random.randint(jax.random.fold_in(key, 102), (block_count,), 0, 6) == 0
    starts_flag = starts_flag | (block_index == 0) | (block_index == block_count - 1)
    doc_label = lax.cummax(jnp.where(starts_flag, block_index, 0), axis=0)
    offsets = jnp.arange(ALIGN, dtype=jnp.int32)
    positions = (block_order[:, None] * ALIGN + offsets[None, :]).reshape(SEQ)
    documents = jnp.broadcast_to(doc_label[block_order][:, None], (block_count, ALIGN)).reshape(SEQ)
    return (positions.astype(jnp.int32), documents.astype(jnp.int32))


def draw_positions(key, part):
    return layout_tables(key)[0]


def draw_doc_ids(key, part):
    return layout_tables(key)[1]


def draw_queries(key, part):
    result = jnp.clip(jax.random.normal(jax.random.fold_in(key, 214), (SEQ, QH, HD), jnp.float32), -4.0, 4.0)
    return result.reshape(SEQ, QH * HD).astype(jnp.bfloat16)


def draw_keys(key, part):
    result = jnp.clip(jax.random.normal(jax.random.fold_in(key, 222), (SEQ, HD), jnp.float32), -4.0, 4.0)
    return result.astype(jnp.bfloat16)


def steps_of(stream_key, shape, pieces, smallest, largest):
    def one(axis_at, parts):
        draws = jax.random.uniform(jax.random.fold_in(jax.random.fold_in(stream_key, 6), axis_at), (parts,), jnp.float32, smallest / len(pieces), largest / len(pieces))
        return jnp.repeat(jnp.exp(draws), shape[axis_at] // parts).reshape((-1,) + (1,) * (len(shape) - axis_at - 1))

    level = one(*pieces[0])
    for cut in pieces[1:]:
        level = level * one(*cut)
    return level


def gaussian(own_key, extent, deviation, reach, shards=(), kind=jnp.bfloat16):
    gain = steps_of(own_key, extent, shards, -0.22, 0.18) if shards else 1.0
    array = jax.random.normal(own_key, extent, jnp.float32) * deviation * gain
    return jnp.minimum(jnp.maximum(array, -reach), reach).astype(kind)


def setup_inputs(seed: int = 0) -> dict:
    key_of = jax.random.split(jax.random.key(seed), 9)
    queries = draw_queries(jax.random.fold_in(key_of[8], 71), 0)
    keys = draw_keys(jax.random.fold_in(key_of[8], 71), 0)
    values = gaussian(key_of[2], (SEQ, HD), 1.0, 6.0, ((0, 64),))
    dout = gaussian(key_of[3], (SEQ, QH * HD), 1.0, 6.0, ((0, 64), (1, 4)))
    positions = draw_positions(jax.random.fold_in(key_of[8], 71), 0)
    doc_ids = draw_doc_ids(jax.random.fold_in(key_of[8], 71), 0)
    w_query = gaussian(key_of[6], (QH * HD, D), (QH * HD) ** -0.5, 0.1875, ((0, 4),))
    w_kv = gaussian(key_of[7], (2 * HD, D), (2 * HD) ** -0.5, 0.375, ((1, 4),))
    return dict(queries=queries, keys=keys, values=values, dout=dout, positions=positions, doc_ids=doc_ids, w_query=w_query, w_kv=w_kv)


def reference(queries, keys, values, dout, positions, doc_ids, w_query, w_kv):
    inv_root = 1.0 / math.sqrt(HD)
    block_rows = math.gcd(SEQ, 512)
    key_rows = keys.astype(jnp.float32)
    value_rows = values.astype(jnp.float32)

    def one_block(totals, block_number):
        key_sum, value_sum = totals
        first_row = (block_number * block_rows).astype(jnp.int32)
        query_rows = lax.dynamic_slice_in_dim(queries, first_row, block_rows, 0).astype(jnp.float32).reshape(block_rows, QH, HD)
        dout_rows = lax.dynamic_slice_in_dim(dout, first_row, block_rows, 0).astype(jnp.float32).reshape(block_rows, QH, HD)
        row_positions = lax.dynamic_slice_in_dim(positions, first_row, block_rows, 0)
        row_docs = lax.dynamic_slice_in_dim(doc_ids, first_row, block_rows, 0)
        allowed = (row_docs[:, None] == doc_ids[None, :]) & (positions[None, :] <= row_positions[:, None])
        scores = jnp.einsum('qhd,kd->hqk', query_rows, key_rows) * inv_root
        scores = jnp.where(allowed[None], scores, -1e+30)
        row_max = lax.optimization_barrier(jnp.max(scores, axis=-1, keepdims=True))
        row_total = lax.optimization_barrier(jnp.sum(jnp.where(allowed[None], jnp.exp(scores - row_max), 0.0), axis=-1, keepdims=True))
        log_total = row_max + jnp.log(row_total)
        probs = jnp.where(allowed[None], jnp.exp(scores - log_total), 0.0)
        output = jnp.einsum('hqk,kd->hqd', probs, value_rows)
        row_delta = jnp.einsum('qhd,hqd->hq', dout_rows, output)
        probs_low = lax.optimization_barrier(probs.astype(jnp.bfloat16)).astype(jnp.float32)
        value_sum = value_sum + jnp.einsum('hqk,qhd->kd', probs_low, dout_rows)
        dprob = jnp.einsum('qhd,kd->hqk', dout_rows, value_rows)
        dscore = lax.optimization_barrier((probs * (dprob - row_delta[..., None])).astype(jnp.bfloat16)).astype(jnp.float32)
        query_grad = (jnp.einsum('hqk,kd->qhd', dscore, key_rows) * inv_root).astype(jnp.bfloat16).reshape(block_rows, QH * HD)
        key_sum = key_sum + jnp.einsum('hqk,qhd->kd', dscore, query_rows)
        return ((key_sum, value_sum), query_grad)
    zero_rows = jnp.zeros((SEQ, HD), jnp.float32)
    (key_sum, value_sum), grads = lax.scan(one_block, (zero_rows, zero_rows), jnp.arange(SEQ // block_rows, dtype=jnp.int32))
    query_grad = grads.reshape(SEQ, QH * HD)
    kv_grads = jnp.concatenate([key_sum * inv_root, value_sum], axis=1).astype(jnp.bfloat16)
    total = jnp.dot(query_grad, w_query, preferred_element_type=jnp.float32) + jnp.dot(kv_grads, w_kv, preferred_element_type=jnp.float32)
    return total.astype(jnp.bfloat16)
```

```python
import math

import jax
import jax.numpy as jnp
from jax import lax
from jax.experimental import pallas as pl
from jax.experimental.pallas import tpu as pltpu
from jax.sharding import Mesh
from jax.sharding import PartitionSpec as P

CTX = ("z", "yl", "x")
HEAD = ("u", "c")
MESH = pl.DeviceIdType.MESH
BF = jnp.bfloat16
F32 = jnp.float32
NEG = -1e30
INV = 1.0 / math.sqrt(128)
LOG2E = 1.4426950408889634
NT = (((1,), (1,)), ((), ()))
NN = (((1,), (0,)), ((), ()))


def mm(a, b, dims=NN):
    return lax.dot_general(a, b, dims, preferred_element_type=F32)


def kernel(
    pos, doc, q, do, k, v, wq, wkv, out,
    Q, DO, KA, V, KT, MQ, MK, meta, tri, S, DP, stat, mloc, stat_all, coef,
    dk, dv, dqs, dqr, pair_s, pair_r, zs, zr, hs, hr, dqf, dqx, W, WK, part_s, part_r,
    q_s, q_r, d_s, d_r, k_s, k_r, v_s, v_r, mq_s, mq_r, mk_s, mk_r, st_s, st_r,
    dq_s, dq_r, z_s, z_r, pr_s, pr_r, h_s, h_r, x_s, x_r, w_s, w_r, pt_s, pt_r, loc,
):
    z, yl, x = lax.axis_index("z"), lax.axis_index("yl"), lax.axis_index("x")
    u, c = lax.axis_index("u"), lax.axis_index("c")
    p = yl * 4 + x

    def plane(d):
        t = (p + d + 8) % 8
        return (z, t // 4, t % 4, u, c)

    def ring(d):
        return ((z + d + 8) % 8, yl, x, u, c)

    mate = (z, yl, x, u, 1 - c)
    side = (z, 1 - yl, x, u, c)
    side_mate = (z, 1 - yl, x, u, 1 - c)
    far = (z, yl, x, 1 - u, c)
    far_mate = (z, yl, x, 1 - u, 1 - c)
    cross = (z, 1 - yl, x, 1 - u, c)

    def rc(src, dst, ss, rs, dev):
        return pltpu.make_async_remote_copy(
            src_ref=src, dst_ref=dst, send_sem=ss, recv_sem=rs, device_id=dev, device_id_type=MESH
        )

    def cols(uu, cc):
        return pl.ds(pl.multiple_of((2 * uu + cc) * 4096, 4096), 4096)

    own = [
        pltpu.make_async_copy(q, Q.at[0], loc.at[0]),
        pltpu.make_async_copy(do, DO.at[0], loc.at[1]),
        pltpu.make_async_copy(k, KA.at[pl.ds(0, 128), pl.ds(0, 128)], loc.at[2]),
        pltpu.make_async_copy(v, V.at[pl.ds(0, 128)], loc.at[3]),
        pltpu.make_async_copy(wq.at[:, cols(u, c)], W.at[pl.ds(0, 256), pl.ds(0, 4096)], loc.at[4]),
        pltpu.make_async_copy(
            wq.at[:, cols(1 - u, c)], W.at[pl.ds(0, 256), pl.ds(4096, 4096)], loc.at[5]
        ),
        pltpu.make_async_copy(wkv, WK, loc.at[6]),
    ]

    lane = lax.broadcasted_iota(jnp.int32, (1, 128), 1)
    r0, r1 = pos[0] // 64, pos[64] // 64
    s0, s1 = doc[0], doc[64]
    rows = [
        jnp.where((lane >= s0) & (lane <= r0), 0.0, NEG),
        jnp.where((lane >= s1) & (lane <= r1), 0.0, NEG),
        jnp.where(lane == r0, 1.0, 0.0),
        jnp.where(lane == r1, 1.0, 0.0),
        jnp.zeros((4, 128), F32),
    ]
    meta_val = jnp.concatenate(rows, axis=0)
    meta[...] = meta_val
    MQ[0] = meta_val
    MK[0] = meta_val
    jj = lax.broadcasted_iota(jnp.int32, (128, 256), 0)
    ii = lax.broadcasted_iota(jnp.int32, (128, 256), 1) % 128
    tri[...] = jnp.where((jj // 64 == ii // 64) & (jj > ii), NEG, 0.0)

    barrier = pltpu.get_barrier_semaphore()
    peers = [plane(d) for d in range(1, 8)] + [ring(d) for d in range(1, 8)]
    peers += [mate, side_mate, far, far_mate, cross]
    for dev in peers:
        pl.semaphore_signal(barrier, inc=1, device_id=dev, device_id_type=MESH)
    for cp in own[:4]:
        cp.start()
    pl.semaphore_wait(barrier, len(peers))

    ORDER = (1, 7, 2, 6, 3, 5, 4)
    gk = {d: rc(k, KA.at[pl.ds(d * 128, 128), pl.ds(0, 128)], k_s.at[d], k_r.at[d], ring(d)) for d in ORDER}
    gv = {d: rc(v, V.at[pl.ds(d * 128, 128)], v_s.at[d], v_r.at[d], ring(d)) for d in ORDER}
    gmk = {d: rc(meta, MK.at[d], mk_s.at[d], mk_r.at[d], ring(d)) for d in ORDER}
    gq = {d: rc(q, Q.at[d], q_s.at[d], q_r.at[d], plane(d)) for d in ORDER}
    gd = {d: rc(do, DO.at[d], d_s.at[d], d_r.at[d], plane(d)) for d in ORDER}
    gmq = {d: rc(meta, MQ.at[d], mq_s.at[d], mq_r.at[d], plane(d)) for d in ORDER}
    for d in ORDER:
        gmk[d].start()
        gk[d].start()
        gv[d].start()
        gmq[d].start()
        gq[d].start()
        gd[d].start()
    wpush = [
        rc(wq.at[:, cols(u, 1 - c)], W.at[pl.ds(256, 256), pl.ds(0, 4096)], w_s.at[0], w_r.at[0], mate),
        rc(wq.at[:, cols(1 - u, 1 - c)], W.at[pl.ds(256, 256), pl.ds(4096, 4096)], w_s.at[1], w_r.at[1], mate),
    ]
    for cp in wpush:
        cp.start()
    for cp in own[4:]:
        cp.start()

    def runs(ref, d, row):
        a = jnp.broadcast_to(ref[d, row : row + 1, :], (64, 128))
        b = jnp.broadcast_to(ref[d, row + 1 : row + 2, :], (64, 128))
        return jnp.concatenate([a, b], axis=0).astype(BF)

    for cp in own[:4]:
        cp.wait()
    for d in range(8):
        if d:
            gmk[d].wait_recv()
            gk[d].wait_recv()
            gv[d].wait_recv()
        at = pl.ds(d * 128, 128)
        KA[at, 128:256] = runs(MK, d, 2)
        KT[:, d * 128 : (d + 1) * 128] = KA[at, 0:128].astype(F32).T.astype(BF)

    def stacked(ref, d):
        return jnp.concatenate([ref[d, :, 0:128], ref[d, :, 128:256]], axis=0)

    def fold(val, op):
        return op(val.reshape(32, 8, 256), axis=0)

    def first(d, carry):
        @pl.when(d > 0)
        def _():
            rc(meta, MQ.at[d], mq_s.at[d], mq_r.at[d], plane(d)).wait_recv()
            rc(q, Q.at[d], q_s.at[d], q_r.at[d], plane(d)).wait_recv()
            rc(do, DO.at[d], d_s.at[d], d_r.at[d], plane(d)).wait_recv()

        bias = runs(MQ, d, 0)
        qa = jnp.concatenate(
            [stacked(Q, d), jnp.concatenate([bias, bias], axis=0)], axis=1
        )
        dd = stacked(DO, d)
        own_tile = jnp.where(d == 0, 1.0, 0.0)
        top = jnp.full((8, 256), -3e38, F32)
        for n in range(4):
            at = pl.ds(n * 256, 256)
            s = mm(KA[at, :], qa, NT)
            if n == 0:
                s = jnp.concatenate([s[0:128] + tri[...] * own_tile, s[128:256]], axis=0)
            S[d, at, :] = s
            top = jnp.maximum(top, fold(s, jnp.max))
            DP[d, at, :] = mm(V[at, :], dd, NT)
        m = jnp.max(top, axis=0, keepdims=True)
        mc = m * (INV * LOG2E)
        total = jnp.zeros((8, 256), F32)
        mixed = jnp.zeros((8, 256), F32)
        for n in range(4):
            at = pl.ds(n * 256, 256)
            e = jnp.exp2(S[d, at, :] * (INV * LOG2E) - mc)
            S[d, at, :] = e
            total = total + fold(e, jnp.sum)
            mixed = mixed + fold(e * DP[d, at, :], jnp.sum)
        total = jnp.sum(total, axis=0, keepdims=True)
        mixed = jnp.sum(mixed, axis=0, keepdims=True)
        mloc[pl.ds(d, 1), :] = m * INV
        stat[0, pl.ds(d, 1), :] = m * INV + jnp.log(total)
        stat[1, pl.ds(d, 1), :] = mixed / total
        return carry

    lax.fori_loop(0, 8, first, 0)

    gs = {d: rc(stat, stat_all.at[d], st_s.at[d], st_r.at[d], plane(d)) for d in ORDER}
    for d in ORDER:
        gs[d].start()
    lses, deltas = [stat[0]], [stat[1]]
    for d in range(1, 8):
        gs[d].wait_recv()
        for row, into in ((0, lses), (1, deltas)):
            a = stat_all[d, row]
            into.append(jnp.concatenate([a[8 - d :], a[: 8 - d]], axis=0))
    big = lses[0]
    for a in lses[1:]:
        big = jnp.maximum(big, a)
    tot = jnp.zeros((8, 256), F32)
    mix = jnp.zeros((8, 256), F32)
    for a, b in zip(lses, deltas):
        w = jnp.exp(a - big)
        tot = tot + w
        mix = mix + w * b
    coef[0] = jnp.exp(mloc[...] - (big + jnp.log(tot)))
    coef[1] = mix / tot

    dk[...] = jnp.zeros_like(dk)
    dv[...] = jnp.zeros_like(dv)

    def second(d, carry):
        f = coef[0, pl.ds(d, 1), :]
        delta = coef[1, pl.ds(d, 1), :]
        qq = stacked(Q, d)
        dd = stacked(DO, d)
        dqt = jnp.zeros((128, 256), F32)
        for n in range(4):
            at = pl.ds(n * 256, 256)
            pn = S[d, at, :] * f
            ds = (pn * (DP[d, at, :] - delta)).astype(BF)
            dv[at, :] += mm(pn.astype(BF), dd)
            dk[at, :] += mm(ds, qq)
            dqt = dqt + mm(KT[:, n * 256 : (n + 1) * 256], ds)
        dqs[d] = dqt.T.astype(BF)

        @pl.when(d > 0)
        def _():
            rc(dqs.at[d], dqr.at[d], dq_s.at[d], dq_r.at[d], plane(-d)).start()

        return carry

    lax.fori_loop(0, 8, second, 0)

    first_core = c == 0
    pair_s[...] = jnp.where(first_core, dv[...], dk[...]).astype(BF)
    pair = rc(pair_s, pair_r, pr_s, pr_r, mate)
    pair.start()

    dqsum = dqs[0].astype(F32)
    for d in range(1, 8):
        rc(dqs.at[d], dqr.at[d], dq_s.at[d], dq_r.at[d], plane(-d)).wait_recv()
        dqsum = dqsum + dqr[d].astype(F32)
    dqsum = (dqsum * INV).astype(BF)
    dqf[:, 0:128] = dqsum[0:128]
    dqf[:, 128:256] = dqsum[128:256]
    gx = [
        rc(dqf, dqx.at[i], x_s.at[i], x_r.at[i], dev)
        for i, dev in enumerate((mate, side, side_mate))
    ]
    for cp in (gx[1], gx[2], gx[0]):
        cp.start()

    pair.wait_recv()
    for d in range(8):
        at = pl.ds(d * 128, 128)
        zs[d] = (jnp.where(first_core, dk[at, :], dv[at, :]) + pair_r[at, :].astype(F32)).astype(BF)
    gz = {d: rc(zs.at[d], zr.at[d], z_s.at[d], z_r.at[d], ring(-d)) for d in ORDER}
    for d in ORDER:
        gz[d].start()

    for cp in wpush:
        cp.wait_recv()
    for cp in own[4:]:
        cp.wait()
    gx[1].wait_recv()
    gx[2].wait_recv()
    side_dq = jnp.concatenate([dqx[1], dqx[2]], axis=1)

    def send_part(n, carry):
        col = pl.multiple_of(4096 + n * 512, 512)
        part_s[n] = mm(side_dq, W[:, pl.ds(col, 512)]).astype(BF)
        rc(part_s.at[n], part_r.at[n], pt_s.at[n], pt_r.at[n], cross).start()
        return carry

    lax.fori_loop(0, 8, send_part, 0)

    ksum = zs[0].astype(F32)
    for d in range(1, 8):
        gz[d].wait_recv()
        ksum = ksum + zr[d].astype(F32)
    hs[...] = ksum.astype(BF)
    gh = [
        rc(hs, hr.at[i], h_s.at[i], h_r.at[i], dev)
        for i, dev in enumerate((mate, far, far_mate))
    ]
    for cp in gh:
        cp.start()
    for cp in gh:
        cp.wait_recv()
    mine = hs[...].astype(F32) + hr[1].astype(F32)
    others = hr[0].astype(F32) + hr[2].astype(F32)
    dk_all = (jnp.where(first_core, mine, others) * INV).astype(BF)
    dv_all = jnp.where(first_core, others, mine).astype(BF)
    kvg = jnp.concatenate([dk_all, dv_all], axis=1)

    gx[0].wait_recv()
    own_dq = jnp.concatenate([dqf[...], dqx[0]], axis=1)

    def finish(n, carry):
        col = pl.multiple_of(n * 512, 512)
        acc = mm(own_dq, W[:, pl.ds(col, 512)]) + mm(kvg, WK[:, pl.ds(col, 512)])
        rc(part_s.at[n], part_r.at[n], pt_s.at[n], pt_r.at[n], cross).wait_recv()
        out[:, pl.ds(col, 512)] = (acc + part_r[n].astype(F32)).astype(BF)
        return carry

    lax.fori_loop(0, 8, finish, 0)

    for d in ORDER:
        for g in (gk, gv, gmk, gq, gd, gmq, gs, gz):
            g[d].wait_send()
        rc(dqs.at[d], dqr.at[d], dq_s.at[d], dq_r.at[d], plane(-d)).wait_send()
    for cp in wpush + gx + gh + [pair]:
        cp.wait_send()
    for n in range(8):
        rc(part_s.at[n], part_r.at[n], pt_s.at[n], pt_r.at[n], cross).wait_send()


def on_device(queries, keys, values, dout, positions, doc_ids, w_query, w_kv):
    anys = pl.BlockSpec(memory_space=pl.ANY)
    smem = pl.BlockSpec(memory_space=pltpu.SMEM)
    V = pltpu.VMEM
    dma = pltpu.SemaphoreType.DMA
    scratch = [
        V((8, 128, 256), BF), V((8, 128, 256), BF), V((1024, 256), BF), V((1024, 128), BF),
        V((128, 1024), BF), V((8, 8, 128), F32), V((8, 8, 128), F32), V((8, 128), F32),
        V((128, 256), F32), V((8, 1024, 256), F32), V((8, 1024, 256), F32),
        V((2, 8, 256), F32), V((8, 256), F32), V((8, 2, 8, 256), F32), V((2, 8, 256), F32),
        V((1024, 128), F32), V((1024, 128), F32), V((8, 256, 128), BF), V((8, 256, 128), BF),
        V((1024, 128), BF), V((1024, 128), BF), V((8, 128, 128), BF), V((8, 128, 128), BF),
        V((128, 128), BF), V((3, 128, 128), BF), V((128, 256), BF), V((3, 128, 256), BF),
        V((512, 8192), BF), V((256, 4096), BF), V((8, 128, 512), BF), V((8, 128, 512), BF),
    ]
    scratch += [dma((8,))] * 18
    scratch += [dma, dma, dma((3,)), dma((3,)), dma((3,)), dma((3,)), dma((2,)), dma((2,))]
    scratch += [dma((8,)), dma((8,)), dma((7,))]
    return pl.pallas_call(
        kernel,
        out_shape=jax.ShapeDtypeStruct((128, 4096), BF),
        in_specs=[smem, smem] + [anys] * 6,
        out_specs=pl.BlockSpec(memory_space=pltpu.VMEM),
        scratch_shapes=scratch,
        compiler_params=pltpu.CompilerParams(
            collective_id=0, has_side_effects=True, vmem_limit_bytes=60 * 1024 * 1024
        ),
    )(positions, doc_ids, queries, dout, keys, values, w_query, w_kv)


def solution(mesh):
    torus = Mesh(mesh.devices.reshape(8, 2, 4, 2, 2), CTX + HEAD)
    return jax.shard_map(
        on_device,
        mesh=torus,
        in_specs=(
            P(CTX, HEAD),
            P(CTX, None),
            P(CTX, None),
            P(CTX, HEAD),
            P(CTX),
            P(CTX),
            P(HEAD, None),
            P(None, HEAD),
        ),
        out_specs=P(CTX, HEAD),
        check_vma=False,
    )
```

```python
import functools
import math

import jax
import jax.numpy as jnp
from jax import lax
from jax.experimental import pallas as pl
from jax.experimental.pallas import tpu as pltpu
from jax.sharding import Mesh
from jax.sharding import PartitionSpec as P

CTX = ("z", "yl", "x")
HEAD = ("u", "c")
MESH = pl.DeviceIdType.MESH
BF = jnp.bfloat16
F32 = jnp.float32
NEG = -1e30
INV = 1.0 / math.sqrt(128)
LOG2E = 1.4426950408889634
NT = (((1,), (1,)), ((), ()))
NN = (((1,), (0,)), ((), ()))


def mm(a, b, dims=NN):
    return lax.dot_general(a, b, dims, preferred_element_type=F32)


def kernel(
    pos, doc, q, do, k, v, wq, wkv, out,
    Q, DO, KA, V, KT, MQ, MK, meta, tri, S, DP, stat, mloc, stat_all, coef,
    dk, dv, dqs, dqr, pair_s, pair_r, zs, zr, hs, hr, dqf, dqx, W, WK, acc,
    q_s, q_r, d_s, d_r, k_s, k_r, v_s, v_r, mq_s, mq_r, mk_s, mk_r, st_s, st_r,
    dq_s, dq_r, z_s, z_r, pr_s, pr_r, h_s, h_r, x_s, x_r, w_s, w_r, cs, cr, fs, fr, loc,
):
    z, yl, x = lax.axis_index("z"), lax.axis_index("yl"), lax.axis_index("x")
    u, c = lax.axis_index("u"), lax.axis_index("c")
    p = yl * 4 + x

    def plane(d):
        t = (p + d + 8) % 8
        return (z, t // 4, t % 4, u, c)

    def ring(d):
        return ((z + d + 8) % 8, yl, x, u, c)

    mate = (z, yl, x, u, 1 - c)
    side = (z, 1 - yl, x, u, c)
    left, right = (z, yl, (x + 3) % 4, u, c), (z, yl, (x + 1) % 4, u, c)
    far = (z, yl, x, 1 - u, c)
    far_mate = (z, yl, x, 1 - u, 1 - c)
    cross = (z, 1 - yl, x, 1 - u, c)
    cross_mate = (z, 1 - yl, x, 1 - u, 1 - c)

    def rc(src, dst, ss, rs, dev):
        return pltpu.make_async_remote_copy(
            src_ref=src, dst_ref=dst, send_sem=ss, recv_sem=rs, device_id=dev, device_id_type=MESH
        )

    def cols(uu, cc):
        return pl.ds(pl.multiple_of((2 * uu + cc) * 4096, 4096), 4096)

    own = [
        pltpu.make_async_copy(q, Q.at[0], loc.at[0]),
        pltpu.make_async_copy(do, DO.at[0], loc.at[1]),
        pltpu.make_async_copy(k, KA.at[pl.ds(0, 128), pl.ds(0, 128)], loc.at[2]),
        pltpu.make_async_copy(v, V.at[pl.ds(0, 128)], loc.at[3]),
        pltpu.make_async_copy(wq.at[:, cols(u, c)], W.at[pl.ds(0, 256)], loc.at[4]),
        pltpu.make_async_copy(wkv, WK, loc.at[5]),
    ]

    lane = lax.broadcasted_iota(jnp.int32, (1, 128), 1)
    r0, r1 = pos[0] // 64, pos[64] // 64
    s0, s1 = doc[0], doc[64]
    rows = [
        jnp.where((lane >= s0) & (lane <= r0), 0.0, NEG),
        jnp.where((lane >= s1) & (lane <= r1), 0.0, NEG),
        jnp.where(lane == r0, 1.0, 0.0),
        jnp.where(lane == r1, 1.0, 0.0),
        jnp.zeros((4, 128), F32),
    ]
    meta_val = jnp.concatenate(rows, axis=0)
    meta[...] = meta_val
    MQ[0] = meta_val
    MK[0] = meta_val
    jj = lax.broadcasted_iota(jnp.int32, (128, 256), 0)
    ii = lax.broadcasted_iota(jnp.int32, (128, 256), 1) % 128
    tri[...] = jnp.where((jj // 64 == ii // 64) & (jj > ii), NEG, 0.0)

    barrier = pltpu.get_barrier_semaphore()
    peers = [plane(d) for d in range(1, 8)] + [ring(d) for d in range(1, 8)]
    peers += [mate, far, far_mate, cross, cross_mate]
    for dev in peers:
        pl.semaphore_signal(barrier, inc=1, device_id=dev, device_id_type=MESH)
    for cp in own[:4]:
        cp.start()
    pl.semaphore_wait(barrier, len(peers))

    ORDER = (1, 7, 2, 6, 3, 5, 4)
    gk = {d: rc(k, KA.at[pl.ds(d * 128, 128), pl.ds(0, 128)], k_s.at[d], k_r.at[d], ring(d)) for d in ORDER}
    gv = {d: rc(v, V.at[pl.ds(d * 128, 128)], v_s.at[d], v_r.at[d], ring(d)) for d in ORDER}
    gmk = {d: rc(meta, MK.at[d], mk_s.at[d], mk_r.at[d], ring(d)) for d in ORDER}
    gq = {d: rc(q, Q.at[d], q_s.at[d], q_r.at[d], plane(d)) for d in ORDER}
    gd = {d: rc(do, DO.at[d], d_s.at[d], d_r.at[d], plane(d)) for d in ORDER}
    gmq = {d: rc(meta, MQ.at[d], mq_s.at[d], mq_r.at[d], plane(d)) for d in ORDER}
    for d in ORDER:
        gmk[d].start()
        gk[d].start()
        gv[d].start()
        gmq[d].start()
        gq[d].start()
        gd[d].start()
    def colors(yy):
        return ((x + 2 * yy) % 4, (z + 2 * yy) % 4, (x + 2 * z) % 4, (z + 2 * x) % 4)

    def sub(part, color, base=0):
        return pl.ds(pl.multiple_of(base + part * 1024 + color * 256, 256), 256)

    mine_c, theirs_c = colors(yl), colors(1 - yl)
    over = []
    for f in range(4):
        at = [(2 * (1 - u) + cc) * 4096 for cc in (c, 1 - c)]
        into = sub(f, theirs_c[f])
        over.append((
            rc(wq.at[:, sub(f, theirs_c[f], at[0])], W.at[pl.ds(512, 256), into], cs.at[f, 0], cr.at[f, 0], cross),
            rc(wq.at[:, sub(f, theirs_c[f], at[1])], W.at[pl.ds(768, 256), into], cs.at[f, 1], cr.at[f, 1], cross_mate),
        ))
    for pair_of in over:
        for cp in pair_of:
            cp.start()

    whole, upper, lower = pl.ds(512, 512), pl.ds(512, 256), pl.ds(768, 256)
    xs = [(right, whole), (left, whole)]
    zz = [(ring(1), whole), (ring(-1), whole)]
    routes = (
        xs + [(side, whole)],
        zz + [(side, whole)],
        xs + [(ring(1), upper), (ring(-1), lower)],
        zz + [(right, upper), (left, lower)],
    )
    relays = []
    for f in range(4):
        at = sub(f, mine_c[f])
        relays.append([
            rc(W.at[part, at], W.at[part, at], fs.at[f, i], fr.at[f, i], dev)
            for i, (dev, part) in enumerate(routes[f])
        ])

    def relay(f):
        for cp in over[f]:
            cp.wait_recv()
        for cp in relays[f]:
            cp.start()

    wpush = [rc(wq.at[:, cols(u, 1 - c)], W.at[pl.ds(256, 256)], w_s, w_r, mate)]
    for cp in wpush:
        cp.start()
    for cp in own[4:]:
        cp.start()

    def runs(ref, d, row):
        a = jnp.broadcast_to(ref[d, row : row + 1, :], (64, 128))
        b = jnp.broadcast_to(ref[d, row + 1 : row + 2, :], (64, 128))
        return jnp.concatenate([a, b], axis=0).astype(BF)

    for cp in own[:4]:
        cp.wait()
    for d in range(8):
        if d:
            gmk[d].wait_recv()
            gk[d].wait_recv()
            gv[d].wait_recv()
        at = pl.ds(d * 128, 128)
        KA[at, 128:256] = runs(MK, d, 2)
        KT[:, d * 128 : (d + 1) * 128] = KA[at, 0:128].astype(F32).T.astype(BF)

    def stacked(ref, d):
        return jnp.concatenate([ref[d, :, 0:128], ref[d, :, 128:256]], axis=0)

    def fold(val, op):
        return op(val.reshape(32, 8, 256), axis=0)

    def slot(g, j):
        owner = g * 4 + (x - j + 4) % 4
        return owner, (p - owner + 8) % 8

    def first(g, j, carry):
        owner, d = slot(g, j)

        @pl.when(d > 0)
        def _():
            rc(meta, MQ.at[d], mq_s.at[d], mq_r.at[d], plane(d)).wait_recv()
            rc(q, Q.at[d], q_s.at[d], q_r.at[d], plane(d)).wait_recv()
            rc(do, DO.at[d], d_s.at[d], d_r.at[d], plane(d)).wait_recv()

        bias = runs(MQ, d, 0)
        qa = jnp.concatenate(
            [stacked(Q, d), jnp.concatenate([bias, bias], axis=0)], axis=1
        )
        dd = stacked(DO, d)
        own_tile = jnp.where(d == 0, 1.0, 0.0)
        top = jnp.full((8, 256), -3e38, F32)
        for n in range(4):
            at = pl.ds(n * 256, 256)
            s = mm(KA[at, :], qa, NT)
            if n == 0:
                s = jnp.concatenate([s[0:128] + tri[...] * own_tile, s[128:256]], axis=0)
            S[d, at, :] = s
            top = jnp.maximum(top, fold(s, jnp.max))
            DP[d, at, :] = mm(V[at, :], dd, NT)
        m = jnp.max(top, axis=0, keepdims=True)
        mc = m * (INV * LOG2E)
        total = jnp.zeros((8, 256), F32)
        mixed = jnp.zeros((8, 256), F32)
        for n in range(4):
            at = pl.ds(n * 256, 256)
            e = jnp.exp2(S[d, at, :] * (INV * LOG2E) - mc)
            S[d, at, :] = e
            total = total + fold(e, jnp.sum)
            mixed = mixed + fold(e * DP[d, at, :], jnp.sum)
        total = jnp.sum(total, axis=0, keepdims=True)
        mixed = jnp.sum(mixed, axis=0, keepdims=True)
        mloc[g, pl.ds(owner - g * 4, 1), :] = m * INV
        stat[g, pl.ds(owner - g * 4, 1), :] = m * INV + jnp.log(total)
        stat[g, pl.ds(owner - g * 4 + 4, 1), :] = mixed / total
        return carry

    gs = [
        {d: rc(stat.at[g], stat_all.at[d, g], st_s.at[d, g], st_r.at[d, g], plane(d)) for d in ORDER}
        for g in range(2)
    ]
    relay(0)
    for g in range(2):
        lax.fori_loop(0, 4, functools.partial(first, g), 0)
        for d in ORDER:
            gs[g][d].start()
        relay(1 + g)

    def merge(g):
        parts = [stat[g]]
        for d in range(1, 8):
            gs[g][d].wait_recv()
            parts.append(stat_all[d, g])
        big = parts[0][0:4]
        for a in parts[1:]:
            big = jnp.maximum(big, a[0:4])
        tot = jnp.zeros((4, 256), F32)
        mix = jnp.zeros((4, 256), F32)
        for a in parts:
            w = jnp.exp(a[0:4] - big)
            tot = tot + w
            mix = mix + w * a[4:8]
        coef[g, 0:4, :] = jnp.exp(mloc[g] - (big + jnp.log(tot)))
        coef[g, 4:8, :] = mix / tot

    dk[...] = jnp.zeros_like(dk)
    dv[...] = jnp.zeros_like(dv)

    def second(g, j, carry):
        owner, d = slot(g, j)
        f = coef[g, pl.ds(owner - g * 4, 1), :]
        delta = coef[g, pl.ds(owner - g * 4 + 4, 1), :]
        qq = stacked(Q, d)
        dd = stacked(DO, d)
        dqt = jnp.zeros((128, 256), F32)
        for n in range(4):
            at = pl.ds(n * 256, 256)
            pn = S[d, at, :] * f
            ds = (pn * (DP[d, at, :] - delta)).astype(BF)
            dv[at, :] += mm(pn.astype(BF), dd)
            dk[at, :] += mm(ds, qq)
            dqt = dqt + mm(KT[:, n * 256 : (n + 1) * 256], ds)
        dqs[d] = dqt.T.astype(BF)

        @pl.when(d > 0)
        def _():
            rc(dqs.at[d], dqr.at[d], dq_s.at[d], dq_r.at[d], plane(-d)).start()

        return carry

    for g in range(2):
        merge(g)
        lax.fori_loop(0, 4, functools.partial(second, g), 0)
        if g == 0:
            relay(3)

    first_core = c == 0
    pair_s[...] = jnp.where(first_core, dv[...], dk[...]).astype(BF)
    pair = rc(pair_s, pair_r, pr_s, pr_r, mate)
    pair.start()

    dqsum = dqs[0].astype(F32)
    for d in range(1, 8):
        rc(dqs.at[d], dqr.at[d], dq_s.at[d], dq_r.at[d], plane(-d)).wait_recv()
        dqsum = dqsum + dqr[d].astype(F32)
    dqsum = (dqsum * INV).astype(BF)
    dqf[:, 0:128] = dqsum[0:128]
    dqf[:, 128:256] = dqsum[128:256]
    gx = [
        rc(dqf, dqx.at[i], x_s.at[i], x_r.at[i], dev)
        for i, dev in enumerate((mate, far, far_mate))
    ]
    for cp in (gx[2], gx[1], gx[0]):
        cp.start()

    pair.wait_recv()
    for d in range(8):
        at = pl.ds(d * 128, 128)
        zs[d] = (jnp.where(first_core, dk[at, :], dv[at, :]) + pair_r[at, :].astype(F32)).astype(BF)
    gz = {d: rc(zs.at[d], zr.at[d], z_s.at[d], z_r.at[d], ring(-d)) for d in ORDER}
    for d in ORDER:
        gz[d].start()

    for cp in wpush:
        cp.wait_recv()
    for cp in own[4:]:
        cp.wait()
    for group in relays:
        for cp in group:
            cp.wait_recv()
    for cp in gx:
        cp.wait_recv()
    all_dq = jnp.concatenate([dqf[...], dqx[0], dqx[1], dqx[2]], axis=1)

    def query_part(n, carry):
        col = pl.ds(pl.multiple_of(n * 512, 512), 512)
        acc[:, col] = mm(all_dq, W[:, col])
        return carry

    lax.fori_loop(0, 8, query_part, 0)

    ksum = zs[0].astype(F32)
    for d in range(1, 8):
        gz[d].wait_recv()
        ksum = ksum + zr[d].astype(F32)
    hs[...] = ksum.astype(BF)
    gh = [
        rc(hs, hr.at[i], h_s.at[i], h_r.at[i], dev)
        for i, dev in enumerate((mate, far, far_mate))
    ]
    for cp in gh:
        cp.start()
    for cp in gh:
        cp.wait_recv()
    mine = hs[...].astype(F32) + hr[1].astype(F32)
    others = hr[0].astype(F32) + hr[2].astype(F32)
    dk_all = (jnp.where(first_core, mine, others) * INV).astype(BF)
    dv_all = jnp.where(first_core, others, mine).astype(BF)
    kvg = jnp.concatenate([dk_all, dv_all], axis=1)

    def finish(n, carry):
        col = pl.ds(pl.multiple_of(n * 512, 512), 512)
        out[:, col] = (acc[:, col] + mm(kvg, WK[:, col])).astype(BF)
        return carry

    lax.fori_loop(0, 8, finish, 0)

    for d in ORDER:
        for g in (gk, gv, gmk, gq, gd, gmq, gs[0], gs[1], gz):
            g[d].wait_send()
        rc(dqs.at[d], dqr.at[d], dq_s.at[d], dq_r.at[d], plane(-d)).wait_send()
    for cp in wpush + gx + gh + [pair]:
        cp.wait_send()
    for f in range(4):
        for cp in relays[f] + list(over[f]):
            cp.wait_send()


def on_device(queries, keys, values, dout, positions, doc_ids, w_query, w_kv):
    anys = pl.BlockSpec(memory_space=pl.ANY)
    smem = pl.BlockSpec(memory_space=pltpu.SMEM)
    V = pltpu.VMEM
    dma = pltpu.SemaphoreType.DMA
    scratch = [
        V((8, 128, 256), BF), V((8, 128, 256), BF), V((1024, 256), BF), V((1024, 128), BF),
        V((128, 1024), BF), V((8, 8, 128), F32), V((8, 8, 128), F32), V((8, 128), F32),
        V((128, 256), F32), V((8, 1024, 256), F32), V((8, 1024, 256), F32),
        V((2, 8, 256), F32), V((2, 4, 256), F32), V((8, 2, 8, 256), F32), V((2, 8, 256), F32),
        V((1024, 128), F32), V((1024, 128), F32), V((8, 256, 128), BF), V((8, 256, 128), BF),
        V((1024, 128), BF), V((1024, 128), BF), V((8, 128, 128), BF), V((8, 128, 128), BF),
        V((128, 128), BF), V((3, 128, 128), BF), V((128, 256), BF), V((3, 128, 256), BF),
        V((1024, 4096), BF), V((256, 4096), BF), V((128, 4096), F32),
    ]
    scratch += [dma((8,))] * 12 + [dma((8, 2))] * 2 + [dma((8,))] * 4
    scratch += [dma, dma, dma((3,)), dma((3,)), dma((3,)), dma((3,)), dma, dma]
    scratch += [dma((4, 2)), dma((4, 2)), dma((4, 4)), dma((4, 4)), dma((6,))]
    return pl.pallas_call(
        kernel,
        out_shape=jax.ShapeDtypeStruct((128, 4096), BF),
        in_specs=[smem, smem] + [anys] * 6,
        out_specs=pl.BlockSpec(memory_space=pltpu.VMEM),
        scratch_shapes=scratch,
        compiler_params=pltpu.CompilerParams(
            collective_id=0, has_side_effects=True, vmem_limit_bytes=60 * 1024 * 1024
        ),
    )(positions, doc_ids, queries, dout, keys, values, w_query, w_kv)


def solution(mesh):
    torus = Mesh(mesh.devices.reshape(8, 2, 4, 2, 2), CTX + HEAD)
    return jax.shard_map(
        on_device,
        mesh=torus,
        in_specs=(
            P(CTX, HEAD),
            P(CTX, None),
            P(CTX, None),
            P(CTX, HEAD),
            P(CTX),
            P(CTX),
            P(HEAD, None),
            P(None, HEAD),
        ),
        out_specs=P(CTX, HEAD),
        check_vma=False,
    )
```

```python
import functools
import math

import jax
import jax.numpy as jnp
from jax import lax
from jax.experimental import pallas as pl
from jax.experimental.pallas import tpu as pltpu
from jax.sharding import Mesh
from jax.sharding import PartitionSpec as P

CTX = ("z", "yl", "x")
HEAD = ("u", "c")
MESH = pl.DeviceIdType.MESH
BF = jnp.bfloat16
F32 = jnp.float32
NEG = -1e30
INV = 1.0 / math.sqrt(128)
LOG2E = 1.4426950408889634
NT = (((1,), (1,)), ((), ()))
NN = (((1,), (0,)), ((), ()))


def mm(a, b, dims=NN):
    return lax.dot_general(a, b, dims, preferred_element_type=F32)


def kernel(
    pos, doc, q, do, k, v, wq, wkv, out,
    QD, KV, OH, KT, MQ, MK, meta, tri, S, DP, stat, mloc, stat_all, coef,
    dk, dv, dqs, dqr, pair_s, pair_r, zs, zr, hs, hr, dqf, dqx, W, WK, acc,
    q_s, q_r, d_s, d_r, k_s, k_r, v_s, v_r, mq_s, mq_r, mk_s, mk_r, st_s, st_r,
    dq_s, dq_r, z_s, z_r, pr_s, pr_r, h_s, h_r, x_s, x_r, w_s, w_r, cs, cr, fs, fr, loc,
):
    z, yl, x = lax.axis_index("z"), lax.axis_index("yl"), lax.axis_index("x")
    u, c = lax.axis_index("u"), lax.axis_index("c")

    def plane(d):
        return (z, (yl + d // 4) % 2, (x + d % 4) % 4, u, c)

    def owner_of(d):
        return (z, (yl + d // 4) % 2, (x + 4 - d % 4) % 4, u, c)

    def ring(d):
        return ((z + d + 8) % 8, yl, x, u, c)

    mate = (z, yl, x, u, 1 - c)
    side = (z, 1 - yl, x, u, c)
    left, right = (z, yl, (x + 3) % 4, u, c), (z, yl, (x + 1) % 4, u, c)
    far = (z, yl, x, 1 - u, c)
    far_mate = (z, yl, x, 1 - u, 1 - c)
    cross = (z, 1 - yl, x, 1 - u, c)
    cross_mate = (z, 1 - yl, x, 1 - u, 1 - c)

    def rc(src, dst, ss, rs, dev):
        return pltpu.make_async_remote_copy(
            src_ref=src, dst_ref=dst, send_sem=ss, recv_sem=rs, device_id=dev, device_id_type=MESH
        )

    def cols(uu, cc):
        return pl.ds(pl.multiple_of((2 * uu + cc) * 4096, 4096), 4096)

    own = [
        pltpu.make_async_copy(q, QD.at[0, 0], loc.at[0]),
        pltpu.make_async_copy(do, QD.at[0, 1], loc.at[1]),
        pltpu.make_async_copy(k, KV.at[0, 0], loc.at[2]),
        pltpu.make_async_copy(v, KV.at[1, 0], loc.at[3]),
        pltpu.make_async_copy(wq.at[:, cols(u, c)], W.at[pl.ds(0, 256)], loc.at[4]),
        pltpu.make_async_copy(wkv, WK, loc.at[5]),
    ]

    lane = lax.broadcasted_iota(jnp.int32, (1, 128), 1)
    r0, r1 = pos[0] // 64, pos[64] // 64
    s0, s1 = doc[0], doc[64]
    rows = [
        jnp.where((lane >= s0) & (lane <= r0), 0.0, NEG),
        jnp.where((lane >= s1) & (lane <= r1), 0.0, NEG),
        jnp.where(lane == r0, 1.0, 0.0),
        jnp.where(lane == r1, 1.0, 0.0),
        jnp.zeros((4, 128), F32),
    ]
    meta_val = jnp.concatenate(rows, axis=0)
    meta[...] = meta_val
    MQ[0] = meta_val
    MK[0] = meta_val
    jj = lax.broadcasted_iota(jnp.int32, (128, 256), 0)
    ii = lax.broadcasted_iota(jnp.int32, (128, 256), 1) % 128
    tri[...] = jnp.where((jj // 64 == ii // 64) & (jj > ii), NEG, 0.0)

    barrier = pltpu.get_barrier_semaphore()
    peers = [plane(d) for d in range(1, 8)] + [ring(d) for d in range(1, 8)]
    peers += [mate, far, far_mate, cross, cross_mate]
    for dev in peers:
        pl.semaphore_signal(barrier, inc=1, device_id=dev, device_id_type=MESH)
    for cp in own[:4]:
        cp.start()
    pl.semaphore_wait(barrier, len(peers))

    ORDER = (1, 7, 2, 6, 3, 5, 4)
    gk = {d: rc(k, KV.at[c, d], k_s.at[d], k_r.at[d], ring(d)) for d in ORDER}
    gv = {d: rc(v, KV.at[c, d], k_s.at[d], k_r.at[d], ring(d)) for d in ORDER}
    gkv = {d: rc(KV.at[c, d], KV.at[c, d], v_s.at[d], v_r.at[d], mate) for d in ORDER}
    gmk = {d: rc(meta, MK.at[d], mk_s.at[d], mk_r.at[d], ring(d)) for d in ORDER}
    gmq = {d: rc(meta, MQ.at[d], mq_s.at[d], mq_r.at[d], plane(d)) for d in ORDER}

    def qd(i, src, d, dev):
        sems = (q_s, q_r) if i == 0 else (d_s, d_r)
        return rc(src, QD.at[d, i], sems[0].at[d], sems[1].at[d], dev)

    gq = {
        1: (qd(0, q, 1, right), qd(1, do, 1, right)),
        3: (qd(0, q, 3, left), qd(1, do, 3, left)),
        4: (qd(0, q, 4, side), qd(1, do, 4, side)),
        2: (qd(0, QD.at[1, 0], 2, right), qd(1, QD.at[3, 1], 2, left)),
        5: (qd(0, QD.at[4, 0], 5, right), qd(1, QD.at[4, 1], 5, right)),
        7: (qd(0, QD.at[4, 0], 7, left), qd(1, QD.at[4, 1], 7, left)),
        6: (qd(0, QD.at[2, 0], 6, side), qd(1, QD.at[2, 1], 6, side)),
    }

    @pl.when(c == 0)
    def _():
        for d in ORDER:
            gk[d].start()

    @pl.when(c == 1)
    def _():
        for d in ORDER:
            gv[d].start()

    for d, i in ((1, 0), (3, 1), (4, 0), (1, 1), (3, 0), (4, 1)):
        gq[d][i].start()
    for d in ORDER:
        gmk[d].start()
        gmq[d].start()

    def colors(yy):
        return ((x + 2 * yy) % 4, (z + 2 * yy) % 4, (x + 2 * z) % 4, (z + 2 * x) % 4)

    def sub(part, color, base=0):
        return pl.ds(pl.multiple_of(base + part * 1024 + color * 256, 256), 256)

    mine_c, theirs_c = colors(yl), colors(1 - yl)
    over = []
    for f in range(4):
        at = [(2 * (1 - u) + cc) * 4096 for cc in (c, 1 - c)]
        into = sub(f, theirs_c[f])
        over.append((
            rc(wq.at[:, sub(f, theirs_c[f], at[0])], W.at[pl.ds(512, 256), into], cs.at[f, 0], cr.at[f, 0], cross),
            rc(wq.at[:, sub(f, theirs_c[f], at[1])], W.at[pl.ds(768, 256), into], cs.at[f, 1], cr.at[f, 1], cross_mate),
        ))
    for pair_of in over:
        for cp in pair_of:
            cp.start()

    whole, upper, lower = pl.ds(512, 512), pl.ds(512, 256), pl.ds(768, 256)
    xs = [(right, whole), (left, whole)]
    zz = [(ring(1), whole), (ring(-1), whole)]
    routes = (
        xs + [(side, whole)],
        zz + [(side, whole)],
        xs + [(ring(1), upper), (ring(-1), lower)],
        zz + [(right, upper), (left, lower)],
    )
    relays = []
    for f in range(4):
        at = sub(f, mine_c[f])
        relays.append([
            rc(W.at[part, at], W.at[part, at], fs.at[f, i], fr.at[f, i], dev)
            for i, (dev, part) in enumerate(routes[f])
        ])

    def relay(f):
        for cp in over[f]:
            cp.wait_recv()
        for cp in relays[f]:
            cp.start()

    wpush = [rc(wq.at[:, cols(u, 1 - c)], W.at[pl.ds(256, 256)], w_s, w_r, mate)]
    for cp in wpush:
        cp.start()
    for cp in own[4:]:
        cp.start()

    def runs(ref, d, row):
        a = jnp.broadcast_to(ref[d, row : row + 1, :], (64, 128))
        b = jnp.broadcast_to(ref[d, row + 1 : row + 2, :], (64, 128))
        return jnp.concatenate([a, b], axis=0).astype(BF)

    def pass_on(*which):
        for d in which:
            gk[d].wait_recv()
            gkv[d].start()

    pass_on(1, 7)
    gq[1][0].wait_recv()
    gq[2][0].start()
    gq[3][1].wait_recv()
    gq[2][1].start()
    gq[4][0].wait_recv()
    gq[5][0].start()
    gq[7][0].start()
    pass_on(2, 6)
    gq[4][1].wait_recv()
    gq[5][1].start()
    gq[7][1].start()
    gq[1][1].wait_recv()
    gq[3][0].wait_recv()
    pass_on(3, 5)
    for i in range(2):
        gq[2][i].wait_recv()
        gq[6][i].start()
    pass_on(4)
    for cp in own[:4]:
        cp.wait()
    for d in (0,) + ORDER:
        if d:
            gmk[d].wait_recv()
            gkv[d].wait_recv()
        at = pl.ds(d * 128, 128)
        OH[at, :] = runs(MK, d, 2)
        KT[:, d * 128 : (d + 1) * 128] = KV[0, d].astype(F32).T.astype(BF)
    for d in ORDER:
        gmq[d].wait_recv()

    def rows_of(i, n):
        return KV[i, 2 * n : 2 * n + 2].reshape(256, 128)

    def stacked(i, d):
        return jnp.concatenate([QD[d, i, :, 0:128], QD[d, i, :, 128:256]], axis=0)

    def fold(val, op):
        return op(val.reshape(32, 8, 256), axis=0)

    def slot(g, dx):
        return (x - dx + 4) % 4, ((yl + g) % 2) * 4 + dx

    def first(g, j, carry):
        owner, d = slot(g, j + (j // 2) * (5 - 2 * j))

        @pl.when(d >= 5)
        def _():
            qd(0, q, d, right).wait_recv()
            qd(1, do, d, right).wait_recv()

        bias = runs(MQ, d, 0)
        qa = jnp.concatenate(
            [stacked(0, d), jnp.concatenate([bias, bias], axis=0)], axis=1
        )
        dd = stacked(1, d)
        own_tile = jnp.where(d == 0, 1.0, 0.0)
        top = jnp.full((8, 256), -3e38, F32)
        for n in range(4):
            at = pl.ds(n * 256, 256)
            s = mm(jnp.concatenate([rows_of(0, n), OH[at, :]], axis=1), qa, NT)
            if n == 0:
                s = jnp.concatenate([s[0:128] + tri[...] * own_tile, s[128:256]], axis=0)
            S[d, at, :] = s
            top = jnp.maximum(top, fold(s, jnp.max))
            DP[d, at, :] = mm(rows_of(1, n), dd, NT)
        m = jnp.max(top, axis=0, keepdims=True)
        mc = m * (INV * LOG2E)
        total = jnp.zeros((8, 256), F32)
        mixed = jnp.zeros((8, 256), F32)
        for n in range(4):
            at = pl.ds(n * 256, 256)
            e = jnp.exp2(S[d, at, :] * (INV * LOG2E) - mc)
            S[d, at, :] = e
            total = total + fold(e, jnp.sum)
            mixed = mixed + fold(e * DP[d, at, :], jnp.sum)
        total = jnp.sum(total, axis=0, keepdims=True)
        mixed = jnp.sum(mixed, axis=0, keepdims=True)
        mloc[g, pl.ds(owner, 1), :] = m * INV
        stat[g, pl.ds(owner, 1), :] = m * INV + jnp.log(total)
        stat[g, pl.ds(owner + 4, 1), :] = mixed / total
        return carry

    gs = [
        {d: rc(stat.at[g], stat_all.at[d, g], st_s.at[d, g], st_r.at[d, g], plane(d)) for d in ORDER}
        for g in range(2)
    ]
    relay(0)
    for g in range(2):
        lax.fori_loop(0, 4, functools.partial(first, g), 0)
        for d in ORDER:
            gs[g][d].start()
        relay(1 + g)

    def merge(g):
        parts = [stat[g]]
        for d in range(1, 8):
            gs[g][d].wait_recv()
            parts.append(stat_all[d, g])
        big = parts[0][0:4]
        for a in parts[1:]:
            big = jnp.maximum(big, a[0:4])
        tot = jnp.zeros((4, 256), F32)
        mix = jnp.zeros((4, 256), F32)
        for a in parts:
            w = jnp.exp(a[0:4] - big)
            tot = tot + w
            mix = mix + w * a[4:8]
        coef[g, 0:4, :] = jnp.exp(mloc[g] - (big + jnp.log(tot)))
        coef[g, 4:8, :] = mix / tot

    dk[...] = jnp.zeros_like(dk)
    dv[...] = jnp.zeros_like(dv)

    def second(g, j, carry):
        owner, d = slot(g, (2 - j) * (1 - j // 2) + (9 - 3 * j) * (j // 2))
        f = coef[g, pl.ds(owner, 1), :]
        delta = coef[g, pl.ds(owner + 4, 1), :]
        qq = stacked(0, d)
        dd = stacked(1, d)
        dqt = jnp.zeros((128, 256), F32)
        for n in range(4):
            at = pl.ds(n * 256, 256)
            pn = S[d, at, :] * f
            ds = (pn * (DP[d, at, :] - delta)).astype(BF)
            dv[at, :] += mm(pn.astype(BF), dd)
            dk[at, :] += mm(ds, qq)
            dqt = dqt + mm(KT[:, n * 256 : (n + 1) * 256], ds)
        dqs[d] = dqt.T.astype(BF)

        @pl.when(d > 0)
        def _():
            rc(dqs.at[d], dqr.at[d], dq_s.at[d], dq_r.at[d], owner_of(d)).start()

        return carry

    for g in range(2):
        merge(g)
        lax.fori_loop(0, 4, functools.partial(second, g), 0)
        if g == 0:
            relay(3)

    first_core = c == 0
    pair_s[...] = jnp.where(first_core, dv[...], dk[...]).astype(BF)
    pair = rc(pair_s, pair_r, pr_s, pr_r, mate)
    pair.start()

    dqsum = dqs[0].astype(F32)
    for d in range(1, 8):
        rc(dqs.at[d], dqr.at[d], dq_s.at[d], dq_r.at[d], owner_of(d)).wait_recv()
        dqsum = dqsum + dqr[d].astype(F32)
    dqsum = (dqsum * INV).astype(BF)
    dqf[:, 0:128] = dqsum[0:128]
    dqf[:, 128:256] = dqsum[128:256]
    gx = [
        rc(dqf, dqx.at[i], x_s.at[i], x_r.at[i], dev)
        for i, dev in enumerate((mate, far, far_mate))
    ]
    for cp in (gx[2], gx[1], gx[0]):
        cp.start()

    pair.wait_recv()
    for d in range(8):
        at = pl.ds(d * 128, 128)
        zs[d] = (jnp.where(first_core, dk[at, :], dv[at, :]) + pair_r[at, :].astype(F32)).astype(BF)
    gz = {d: rc(zs.at[d], zr.at[d], z_s.at[d], z_r.at[d], ring(-d)) for d in ORDER}
    for d in ORDER:
        gz[d].start()

    for cp in wpush:
        cp.wait_recv()
    for cp in own[4:]:
        cp.wait()
    for group in relays:
        for cp in group:
            cp.wait_recv()
    for cp in gx:
        cp.wait_recv()
    all_dq = jnp.concatenate([dqf[...], dqx[0], dqx[1], dqx[2]], axis=1)

    def query_part(n, carry):
        col = pl.ds(pl.multiple_of(n * 512, 512), 512)
        acc[:, col] = mm(all_dq, W[:, col])
        return carry

    lax.fori_loop(0, 8, query_part, 0)

    ksum = zs[0].astype(F32)
    for d in range(1, 8):
        gz[d].wait_recv()
        ksum = ksum + zr[d].astype(F32)
    hs[...] = ksum.astype(BF)
    gh = [
        rc(hs, hr.at[i], h_s.at[i], h_r.at[i], dev)
        for i, dev in enumerate((mate, far, far_mate))
    ]
    for cp in gh:
        cp.start()
    for cp in gh:
        cp.wait_recv()
    mine = hs[...].astype(F32) + hr[1].astype(F32)
    others = hr[0].astype(F32) + hr[2].astype(F32)
    dk_all = (jnp.where(first_core, mine, others) * INV).astype(BF)
    dv_all = jnp.where(first_core, others, mine).astype(BF)
    kvg = jnp.concatenate([dk_all, dv_all], axis=1)

    def finish(n, carry):
        col = pl.ds(pl.multiple_of(n * 512, 512), 512)
        out[:, col] = (acc[:, col] + mm(kvg, WK[:, col])).astype(BF)
        return carry

    lax.fori_loop(0, 8, finish, 0)

    for d in ORDER:
        for g in (gk, gkv, gmk, gmq, gs[0], gs[1], gz):
            g[d].wait_send()
        for cp in gq[d]:
            cp.wait_send()
        rc(dqs.at[d], dqr.at[d], dq_s.at[d], dq_r.at[d], owner_of(d)).wait_send()
    for cp in wpush + gx + gh + [pair]:
        cp.wait_send()
    for f in range(4):
        for cp in relays[f] + list(over[f]):
            cp.wait_send()


def on_device(queries, keys, values, dout, positions, doc_ids, w_query, w_kv):
    anys = pl.BlockSpec(memory_space=pl.ANY)
    smem = pl.BlockSpec(memory_space=pltpu.SMEM)
    V = pltpu.VMEM
    dma = pltpu.SemaphoreType.DMA
    scratch = [
        V((8, 2, 128, 256), BF), V((2, 8, 128, 128), BF), V((1024, 128), BF),
        V((128, 1024), BF), V((8, 8, 128), F32), V((8, 8, 128), F32), V((8, 128), F32),
        V((128, 256), F32), V((8, 1024, 256), F32), V((8, 1024, 256), F32),
        V((2, 8, 256), F32), V((2, 4, 256), F32), V((8, 2, 8, 256), F32), V((2, 8, 256), F32),
        V((1024, 128), F32), V((1024, 128), F32), V((8, 256, 128), BF), V((8, 256, 128), BF),
        V((1024, 128), BF), V((1024, 128), BF), V((8, 128, 128), BF), V((8, 128, 128), BF),
        V((128, 128), BF), V((3, 128, 128), BF), V((128, 256), BF), V((3, 128, 256), BF),
        V((1024, 4096), BF), V((256, 4096), BF), V((128, 4096), F32),
    ]
    scratch += [dma((8,))] * 12 + [dma((8, 2))] * 2 + [dma((8,))] * 4
    scratch += [dma, dma, dma((3,)), dma((3,)), dma((3,)), dma((3,)), dma, dma]
    scratch += [dma((4, 2)), dma((4, 2)), dma((4, 4)), dma((4, 4)), dma((6,))]
    return pl.pallas_call(
        kernel,
        out_shape=pltpu.VMEM((128, 4096), BF),
        in_specs=[smem, smem] + [anys] * 6,
        out_specs=pl.BlockSpec(memory_space=pltpu.VMEM),
        scratch_shapes=scratch,
        compiler_params=pltpu.CompilerParams(
            collective_id=0, has_side_effects=True, vmem_limit_bytes=60 * 1024 * 1024
        ),
    )(positions, doc_ids, queries, dout, keys, values, w_query, w_kv)


def solution(mesh):
    torus = Mesh(mesh.devices.reshape(8, 2, 4, 2, 2), CTX + HEAD)
    return jax.shard_map(
        on_device,
        mesh=torus,
        in_specs=(
            P(CTX, HEAD),
            P(CTX, None),
            P(CTX, None),
            P(CTX, HEAD),
            P(CTX),
            P(CTX),
            P(HEAD, None),
            P(None, HEAD),
        ),
        out_specs=P(CTX, HEAD),
        check_vma=False,
    )
```

```python
import functools
import math

import jax
import jax.numpy as jnp
from jax import lax
from jax.experimental import pallas as pl
from jax.experimental.pallas import tpu as pltpu
from jax.sharding import Mesh
from jax.sharding import PartitionSpec as P

CTX = ("z", "yl", "x")
HEAD = ("u", "c")
MESH = pl.DeviceIdType.MESH
BF = jnp.bfloat16
F32 = jnp.float32
NEG = -1e30
INV = 1.0 / math.sqrt(128)
LOG2E = 1.4426950408889634
NT = (((1,), (1,)), ((), ()))
NN = (((1,), (0,)), ((), ()))


def mm(a, b, dims=NN):
    return lax.dot_general(a, b, dims, preferred_element_type=F32)


def kernel(
    pos, doc, q, do, k, v, wq, wkv, out,
    QD, KV, OH, KT, MQ, MK, meta, tri, S, DP, stat, mloc, stat_all, coef,
    dk, dv, dqs, dqr, pair_s, pair_r, zs, zr, hs, hr, dqf, dqx, W, WK, acc,
    q_s, q_r, d_s, d_r, k_s, k_r, v_s, v_r, mq_s, mq_r, mk_s, mk_r, st_s, st_r,
    dq_s, dq_r, z_s, z_r, pr_s, pr_r, h_s, h_r, x_s, x_r, w_s, w_r, cs, cr, fs, fr, loc,
):
    z, yl, x = lax.axis_index("z"), lax.axis_index("yl"), lax.axis_index("x")
    u, c = lax.axis_index("u"), lax.axis_index("c")

    def plane(d):
        return (z, (yl + d // 4) % 2, (x + d % 4) % 4, u, c)

    def owner_of(d):
        return (z, (yl + d // 4) % 2, (x + 4 - d % 4) % 4, u, c)

    def ring(d):
        return ((z + d + 8) % 8, yl, x, u, c)

    mate = (z, yl, x, u, 1 - c)
    side = (z, 1 - yl, x, u, c)
    left, right = (z, yl, (x + 3) % 4, u, c), (z, yl, (x + 1) % 4, u, c)
    far = (z, yl, x, 1 - u, c)
    far_mate = (z, yl, x, 1 - u, 1 - c)
    cross = (z, 1 - yl, x, 1 - u, c)
    cross_mate = (z, 1 - yl, x, 1 - u, 1 - c)

    def rc(src, dst, ss, rs, dev):
        return pltpu.make_async_remote_copy(
            src_ref=src, dst_ref=dst, send_sem=ss, recv_sem=rs, device_id=dev, device_id_type=MESH
        )

    def cols(uu, cc):
        return pl.ds(pl.multiple_of((2 * uu + cc) * 4096, 4096), 4096)

    own = [
        pltpu.make_async_copy(q, QD.at[0, 0], loc.at[0]),
        pltpu.make_async_copy(do, QD.at[0, 1], loc.at[1]),
        pltpu.make_async_copy(k, KV.at[0, 0], loc.at[2]),
        pltpu.make_async_copy(v, KV.at[1, 0], loc.at[3]),
        pltpu.make_async_copy(wq.at[:, cols(u, c)], W.at[pl.ds(0, 256)], loc.at[4]),
        pltpu.make_async_copy(wkv, WK, loc.at[5]),
    ]

    lane = lax.broadcasted_iota(jnp.int32, (1, 128), 1)
    r0, r1 = pos[0] // 64, pos[64] // 64
    s0, s1 = doc[0], doc[64]
    rows = [
        jnp.where((lane >= s0) & (lane <= r0), 0.0, NEG),
        jnp.where((lane >= s1) & (lane <= r1), 0.0, NEG),
        jnp.where(lane == r0, 1.0, 0.0),
        jnp.where(lane == r1, 1.0, 0.0),
        jnp.zeros((4, 128), F32),
    ]
    meta_val = jnp.concatenate(rows, axis=0)
    meta[...] = meta_val
    MQ[0] = meta_val
    MK[0] = meta_val
    jj = lax.broadcasted_iota(jnp.int32, (128, 256), 0)
    ii = lax.broadcasted_iota(jnp.int32, (128, 256), 1) % 128
    tri[...] = jnp.where((jj // 64 == ii // 64) & (jj > ii), NEG, 0.0)

    barrier = pltpu.get_barrier_semaphore()
    peers = [mate, left, right, side, ring(1), ring(-1), cross, cross_mate]
    for dev in peers:
        pl.semaphore_signal(barrier, inc=1, device_id=dev, device_id_type=MESH)
    for cp in own[:4]:
        cp.start()
    pl.semaphore_wait(barrier, len(peers))

    ORDER = (1, 7, 2, 6, 3, 5, 4)
    up, down = ring(1), ring(-1)
    halves = (pl.ds(0, 64), pl.ds(64, 64))

    def kv_hop(src, d, dev):
        return rc(src, KV.at[c, d], k_s.at[d], k_r.at[d], dev)

    def kv_half(d, half, sem, dev):
        part = halves[half]
        return rc(KV.at[c, d, part], KV.at[c, 4, part], k_s.at[sem], k_r.at[sem], dev)

    gk = {1: kv_hop(k, 1, up), 7: kv_hop(k, 7, down)}
    gv = {1: kv_hop(v, 1, up), 7: kv_hop(v, 7, down)}
    for d in (2, 3):
        gk[d] = kv_hop(KV.at[c, d - 1], d, up)
        gk[8 - d] = kv_hop(KV.at[c, 9 - d], 8 - d, down)
    gk[4] = kv_half(3, 0, 4, up)
    gk[0] = kv_half(5, 1, 0, down)
    gkv = {d: rc(KV.at[c, d], KV.at[c, d], v_s.at[d], v_r.at[d], mate) for d in ORDER}

    def hop(buf, sems, d, dev, src):
        return rc(meta if src == 0 else buf.at[src], buf.at[d], sems[0].at[d], sems[1].at[d], dev)

    mk = (mk_s, mk_r)
    gmk = {d: hop(MK, mk, d, up, d - 1) for d in (1, 2, 3, 4)}
    gmk.update({d: hop(MK, mk, d, down, (d + 1) % 8) for d in (7, 6, 5)})
    mq = (mq_s, mq_r)
    gmq = {1: hop(MQ, mq, 1, right, 0), 3: hop(MQ, mq, 3, left, 0), 4: hop(MQ, mq, 4, side, 0)}
    gmq.update({2: hop(MQ, mq, 2, right, 1), 5: hop(MQ, mq, 5, right, 4)})
    gmq.update({7: hop(MQ, mq, 7, left, 4), 6: hop(MQ, mq, 6, side, 2)})

    def qd(i, src, d, dev):
        sems = (q_s, q_r) if i == 0 else (d_s, d_r)
        return rc(src, QD.at[d, i], sems[0].at[d], sems[1].at[d], dev)

    gq = {
        1: (qd(0, q, 1, right), qd(1, do, 1, right)),
        3: (qd(0, q, 3, left), qd(1, do, 3, left)),
        4: (qd(0, q, 4, side), qd(1, do, 4, side)),
        2: (qd(0, QD.at[1, 0], 2, right), qd(1, QD.at[3, 1], 2, left)),
        5: (qd(0, QD.at[4, 0], 5, right), qd(1, QD.at[4, 1], 5, right)),
        7: (qd(0, QD.at[4, 0], 7, left), qd(1, QD.at[4, 1], 7, left)),
        6: (qd(0, QD.at[2, 0], 6, side), qd(1, QD.at[2, 1], 6, side)),
    }

    @pl.when(c == 0)
    def _():
        gk[1].start()
        gk[7].start()

    @pl.when(c == 1)
    def _():
        gv[1].start()
        gv[7].start()

    for d in (1, 7):
        gmk[d].start()
    for d in (1, 3, 4):
        gmq[d].start()
    for d, i in ((1, 0), (3, 1), (4, 0), (1, 1), (3, 0), (4, 1)):
        gq[d][i].start()

    def colors(yy):
        return ((x + 2 * yy) % 4, (z + 2 * x) % 4, (z + 2 * x) % 4, (z + 2 * yy) % 4)

    def sub(part, color, base=0):
        return pl.ds(pl.multiple_of(base + part * 1024 + color * 256, 256), 256)

    mine_c, theirs_c = colors(yl), colors(1 - yl)
    over = []
    for f in range(4):
        at = [(2 * (1 - u) + cc) * 4096 for cc in (c, 1 - c)]
        into = sub(f, theirs_c[f])
        over.append((
            rc(wq.at[:, sub(f, theirs_c[f], at[0])], W.at[pl.ds(512, 256), into], cs.at[f, 0], cr.at[f, 0], cross),
            rc(wq.at[:, sub(f, theirs_c[f], at[1])], W.at[pl.ds(768, 256), into], cs.at[f, 1], cr.at[f, 1], cross_mate),
        ))
    for pair_of in over:
        for cp in pair_of:
            cp.start()

    whole, upper, lower = pl.ds(512, 512), pl.ds(512, 256), pl.ds(768, 256)
    xs = [(right, whole), (left, whole)]
    zz = [(ring(1), whole), (ring(-1), whole)]
    routes = (
        xs + [(side, whole)],
        zz + [(right, upper), (left, lower)],
        zz + [(right, upper), (left, lower)],
        zz + [(side, whole)],
    )
    relays = []
    for f in range(4):
        at = sub(f, mine_c[f])
        relays.append([
            rc(W.at[part, at], W.at[part, at], fs.at[f, i], fr.at[f, i], dev)
            for i, (dev, part) in enumerate(routes[f])
        ])

    def relay(f):
        for cp in over[f]:
            cp.wait_recv()
        for cp in relays[f]:
            cp.start()

    wpush = [rc(wq.at[:, cols(u, 1 - c)], W.at[pl.ds(256, 256)], w_s, w_r, mate)]
    for cp in wpush:
        cp.start()
    for cp in own[4:]:
        cp.start()

    def runs(ref, d, row):
        a = jnp.broadcast_to(ref[d, row : row + 1, :], (64, 128))
        b = jnp.broadcast_to(ref[d, row + 1 : row + 2, :], (64, 128))
        return jnp.concatenate([a, b], axis=0).astype(BF)

    def pass_on(d, to):
        gmk[d].wait_recv()
        gk[d].wait_recv()
        if to is not None:
            gmk[to].start()
            gk[to].start()
        elif d == 3:
            gmk[4].start()
            gk[4].start()
        else:
            gk[0].start()
        gkv[d].start()

    pass_on(1, 2)
    pass_on(7, 6)
    gmq[1].wait_recv()
    gmq[2].start()
    gq[1][0].wait_recv()
    gq[2][0].start()
    gmq[3].wait_recv()
    gq[3][1].wait_recv()
    gq[2][1].start()
    gmq[4].wait_recv()
    gmq[5].start()
    gmq[7].start()
    gq[4][0].wait_recv()
    gq[5][0].start()
    gq[7][0].start()
    pass_on(2, 3)
    pass_on(6, 5)
    gq[4][1].wait_recv()
    gq[5][1].start()
    gq[7][1].start()
    gq[1][1].wait_recv()
    gq[3][0].wait_recv()
    pass_on(3, None)
    pass_on(5, None)
    gmq[2].wait_recv()
    gmq[6].start()
    for i in range(2):
        gq[2][i].wait_recv()
        gq[6][i].start()
    gmk[4].wait_recv()
    gk[4].wait_recv()
    gk[0].wait_recv()
    gkv[4].start()
    for cp in own[:4]:
        cp.wait()
    for d in (0,) + ORDER:
        if d:
            gkv[d].wait_recv()
        at = pl.ds(d * 128, 128)
        OH[at, :] = runs(MK, d, 2)
        KT[:, d * 128 : (d + 1) * 128] = KV[0, d].astype(F32).T.astype(BF)
    for d in (5, 6, 7):
        gmq[d].wait_recv()

    def rows_of(i, n):
        return KV[i, 2 * n : 2 * n + 2].reshape(256, 128)

    def stacked(i, d):
        return jnp.concatenate([QD[d, i, :, 0:128], QD[d, i, :, 128:256]], axis=0)

    def fold(val, op):
        return op(val.reshape(32, 8, 256), axis=0)

    def slot(g, dx):
        return (x - dx + 4) % 4, ((yl + g) % 2) * 4 + dx

    def first(g, j, carry):
        owner, d = slot(g, j + (j // 2) * (5 - 2 * j))

        @pl.when(d >= 5)
        def _():
            qd(0, q, d, right).wait_recv()
            qd(1, do, d, right).wait_recv()

        bias = runs(MQ, d, 0)
        qa = jnp.concatenate(
            [stacked(0, d), jnp.concatenate([bias, bias], axis=0)], axis=1
        )
        dd = stacked(1, d)
        own_tile = jnp.where(d == 0, 1.0, 0.0)
        top = jnp.full((8, 256), -3e38, F32)
        for n in range(4):
            at = pl.ds(n * 256, 256)
            s = mm(jnp.concatenate([rows_of(0, n), OH[at, :]], axis=1), qa, NT)
            if n == 0:
                s = jnp.concatenate([s[0:128] + tri[...] * own_tile, s[128:256]], axis=0)
            S[d, at, :] = s
            top = jnp.maximum(top, fold(s, jnp.max))
            DP[d, at, :] = mm(rows_of(1, n), dd, NT)
        m = jnp.max(top, axis=0, keepdims=True)
        mc = m * (INV * LOG2E)
        total = jnp.zeros((8, 256), F32)
        mixed = jnp.zeros((8, 256), F32)
        for n in range(4):
            at = pl.ds(n * 256, 256)
            e = jnp.exp2(S[d, at, :] * (INV * LOG2E) - mc)
            S[d, at, :] = e
            total = total + fold(e, jnp.sum)
            mixed = mixed + fold(e * DP[d, at, :], jnp.sum)
        total = jnp.sum(total, axis=0, keepdims=True)
        mixed = jnp.sum(mixed, axis=0, keepdims=True)
        mloc[g, pl.ds(owner, 1), :] = m * INV
        stat[g, pl.ds(owner, 1), :] = m * INV + jnp.log(total)
        stat[g, pl.ds(owner + 4, 1), :] = mixed / total
        return carry

    gs = [
        {d: rc(stat.at[g], stat_all.at[d, g], st_s.at[d, g], st_r.at[d, g], plane(d)) for d in ORDER}
        for g in range(2)
    ]
    relay(0)
    for g in range(2):
        lax.fori_loop(0, 4, functools.partial(first, g), 0)
        for d in ORDER:
            gs[g][d].start()
        relay(1 + g)

    def merge(g):
        parts = [stat[g]]
        for d in range(1, 8):
            gs[g][d].wait_recv()
            parts.append(stat_all[d, g])
        big = parts[0][0:4]
        for a in parts[1:]:
            big = jnp.maximum(big, a[0:4])
        tot = jnp.zeros((4, 256), F32)
        mix = jnp.zeros((4, 256), F32)
        for a in parts:
            w = jnp.exp(a[0:4] - big)
            tot = tot + w
            mix = mix + w * a[4:8]
        coef[g, 0:4, :] = jnp.exp(mloc[g] - (big + jnp.log(tot)))
        coef[g, 4:8, :] = mix / tot

    dk[...] = jnp.zeros_like(dk)
    dv[...] = jnp.zeros_like(dv)

    def second(g, j, carry):
        owner, d = slot(g, (2 - j) * (1 - j // 2) + (9 - 3 * j) * (j // 2))
        f = coef[g, pl.ds(owner, 1), :]
        delta = coef[g, pl.ds(owner + 4, 1), :]
        qq = stacked(0, d)
        dd = stacked(1, d)
        dqt = jnp.zeros((128, 256), F32)
        for n in range(4):
            at = pl.ds(n * 256, 256)
            pn = S[d, at, :] * f
            ds = (pn * (DP[d, at, :] - delta)).astype(BF)
            dv[at, :] += mm(pn.astype(BF), dd)
            dk[at, :] += mm(ds, qq)
            dqt = dqt + mm(KT[:, n * 256 : (n + 1) * 256], ds)
        dqs[d] = dqt.T.astype(BF)

        @pl.when(d > 0)
        def _():
            rc(dqs.at[d], dqr.at[d], dq_s.at[d], dq_r.at[d], owner_of(d)).start()

        return carry

    for g in range(2):
        merge(g)
        lax.fori_loop(0, 4, functools.partial(second, g), 0)
        if g == 0:
            relay(3)

    first_core = c == 0
    pair_s[...] = jnp.where(first_core, dv[...], dk[...]).astype(BF)
    pair = rc(pair_s, pair_r, pr_s, pr_r, mate)
    pair.start()

    dqsum = dqs[0].astype(F32)
    for d in range(1, 8):
        rc(dqs.at[d], dqr.at[d], dq_s.at[d], dq_r.at[d], owner_of(d)).wait_recv()
        dqsum = dqsum + dqr[d].astype(F32)
    dqsum = (dqsum * INV).astype(BF)
    dqf[:, 0:128] = dqsum[0:128]
    dqf[:, 128:256] = dqsum[128:256]
    gx = [
        rc(dqf, dqx.at[i], x_s.at[i], x_r.at[i], dev)
        for i, dev in enumerate((mate, far, far_mate))
    ]
    relays[0][2].wait_recv()
    for cp in (gx[2], gx[1], gx[0]):
        cp.start()

    pair.wait_recv()
    for d in range(8):
        at = pl.ds(d * 128, 128)
        zs[d] = (jnp.where(first_core, dk[at, :], dv[at, :]) + pair_r[at, :].astype(F32)).astype(BF)
    gz = {d: rc(zs.at[d], zr.at[d], z_s.at[d], z_r.at[d], ring(-d)) for d in ORDER}
    for d in ORDER:
        gz[d].start()

    for cp in wpush:
        cp.wait_recv()
    for cp in own[4:]:
        cp.wait()
    for cp in relays[0][:2] + relays[1] + relays[2] + relays[3]:
        cp.wait_recv()
    for cp in gx:
        cp.wait_recv()
    all_dq = jnp.concatenate([dqf[...], dqx[0], dqx[1], dqx[2]], axis=1)

    def query_part(n, carry):
        col = pl.ds(pl.multiple_of(n * 512, 512), 512)
        acc[:, col] = mm(all_dq, W[:, col])
        return carry

    lax.fori_loop(0, 8, query_part, 0)

    ksum = zs[0].astype(F32)
    for d in range(1, 8):
        gz[d].wait_recv()
        ksum = ksum + zr[d].astype(F32)
    hs[...] = ksum.astype(BF)
    gh = [
        rc(hs, hr.at[i], h_s.at[i], h_r.at[i], dev)
        for i, dev in enumerate((mate, far, far_mate))
    ]
    for cp in gh:
        cp.start()
    for cp in gh:
        cp.wait_recv()
    mine = hs[...].astype(F32) + hr[1].astype(F32)
    others = hr[0].astype(F32) + hr[2].astype(F32)
    dk_all = (jnp.where(first_core, mine, others) * INV).astype(BF)
    dv_all = jnp.where(first_core, others, mine).astype(BF)
    kvg = jnp.concatenate([dk_all, dv_all], axis=1)

    def finish(n, carry):
        col = pl.ds(pl.multiple_of(n * 512, 512), 512)
        out[:, col] = (acc[:, col] + mm(kvg, WK[:, col])).astype(BF)
        return carry

    lax.fori_loop(0, 8, finish, 0)

    for d in ORDER:
        for g in (gk, gkv, gmk, gmq, gs[0], gs[1], gz):
            g[d].wait_send()
        for cp in gq[d]:
            cp.wait_send()
        rc(dqs.at[d], dqr.at[d], dq_s.at[d], dq_r.at[d], owner_of(d)).wait_send()
    for cp in wpush + gx + gh + [pair, gk[0]]:
        cp.wait_send()
    for f in range(4):
        for cp in relays[f] + list(over[f]):
            cp.wait_send()


def on_device(queries, keys, values, dout, positions, doc_ids, w_query, w_kv):
    anys = pl.BlockSpec(memory_space=pl.ANY)
    smem = pl.BlockSpec(memory_space=pltpu.SMEM)
    V = pltpu.VMEM
    dma = pltpu.SemaphoreType.DMA
    scratch = [
        V((8, 2, 128, 256), BF), V((2, 8, 128, 128), BF), V((1024, 128), BF),
        V((128, 1024), BF), V((8, 8, 128), F32), V((8, 8, 128), F32), V((8, 128), F32),
        V((128, 256), F32), V((8, 1024, 256), F32), V((8, 1024, 256), F32),
        V((2, 8, 256), F32), V((2, 4, 256), F32), V((8, 2, 8, 256), F32), V((2, 8, 256), F32),
        V((1024, 128), F32), V((1024, 128), F32), V((8, 256, 128), BF), V((8, 256, 128), BF),
        V((1024, 128), BF), V((1024, 128), BF), V((8, 128, 128), BF), V((8, 128, 128), BF),
        V((128, 128), BF), V((3, 128, 128), BF), V((128, 256), BF), V((3, 128, 256), BF),
        V((1024, 4096), BF), V((256, 4096), BF), V((128, 4096), F32),
    ]
    scratch += [dma((8,))] * 12 + [dma((8, 2))] * 2 + [dma((8,))] * 4
    scratch += [dma, dma, dma((3,)), dma((3,)), dma((3,)), dma((3,)), dma, dma]
    scratch += [dma((4, 2)), dma((4, 2)), dma((4, 4)), dma((4, 4)), dma((6,))]
    return pl.pallas_call(
        kernel,
        out_shape=pltpu.VMEM((128, 4096), BF),
        in_specs=[smem, smem] + [anys] * 6,
        out_specs=pl.BlockSpec(memory_space=pltpu.VMEM),
        scratch_shapes=scratch,
        compiler_params=pltpu.CompilerParams(
            collective_id=0, has_side_effects=True, vmem_limit_bytes=60 * 1024 * 1024
        ),
    )(positions, doc_ids, queries, dout, keys, values, w_query, w_kv)


def solution(mesh):
    torus = Mesh(mesh.devices.reshape(8, 2, 4, 2, 2), CTX + HEAD)
    return jax.shard_map(
        on_device,
        mesh=torus,
        in_specs=(
            P(CTX, HEAD),
            P(CTX, None),
            P(CTX, None),
            P(CTX, HEAD),
            P(CTX),
            P(CTX),
            P(HEAD, None),
            P(None, HEAD),
        ),
        out_specs=P(CTX, HEAD),
        check_vma=False,
    )
```

```python
import functools
import math

import jax
import jax.numpy as jnp
from jax import lax
from jax.experimental import pallas as pl
from jax.experimental.pallas import tpu as pltpu
from jax.sharding import Mesh
from jax.sharding import PartitionSpec as P

CTX = ("z", "yl", "x")
HEAD = ("u", "c")
MESH = pl.DeviceIdType.MESH
BF = jnp.bfloat16
F32 = jnp.float32
NEG = -1e30
INV = 1.0 / math.sqrt(128)
LOG2E = 1.4426950408889634
NT = (((1,), (1,)), ((), ()))
NN = (((1,), (0,)), ((), ()))


def mm(a, b, dims=NN):
    return lax.dot_general(a, b, dims, preferred_element_type=F32)


def kernel(
    pos, doc, q, do, k, v, wq, wkv, out,
    QD, KV, OH, KT, MQ, MK, meta, tri, S, DP, stat, mloc, stat_all, coef,
    dk, dv, dqs, dqr, pair_s, pair_r, zs, zr, hs, hr, dqf, dqx, W, WK, acc,
    q_s, q_r, d_s, d_r, k_s, k_r, v_s, v_r, mq_s, mq_r, mk_s, mk_r, st_s, st_r,
    dq_s, dq_r, z_s, z_r, pr_s, pr_r, h_s, h_r, x_s, x_r, w_s, w_r, cs, cr, fs, fr, loc,
):
    z, yl, x = lax.axis_index("z"), lax.axis_index("yl"), lax.axis_index("x")
    u, c = lax.axis_index("u"), lax.axis_index("c")

    def plane(d):
        return (z, (yl + d // 4) % 2, (x + d % 4) % 4, u, c)

    def owner_of(d):
        return (z, (yl + d // 4) % 2, (x + 4 - d % 4) % 4, u, c)

    def ring(d):
        return ((z + d + 8) % 8, yl, x, u, c)

    mate = (z, yl, x, u, 1 - c)
    side = (z, 1 - yl, x, u, c)
    left, right = (z, yl, (x + 3) % 4, u, c), (z, yl, (x + 1) % 4, u, c)
    far = (z, yl, x, 1 - u, c)
    far_mate = (z, yl, x, 1 - u, 1 - c)
    cross = (z, 1 - yl, x, 1 - u, c)
    cross_mate = (z, 1 - yl, x, 1 - u, 1 - c)

    def rc(src, dst, ss, rs, dev):
        return pltpu.make_async_remote_copy(
            src_ref=src, dst_ref=dst, send_sem=ss, recv_sem=rs, device_id=dev, device_id_type=MESH
        )

    def cols(uu, cc):
        return pl.ds(pl.multiple_of((2 * uu + cc) * 4096, 4096), 4096)

    own = [
        pltpu.make_async_copy(q, QD.at[0, 0], loc.at[0]),
        pltpu.make_async_copy(do, QD.at[0, 1], loc.at[1]),
        pltpu.make_async_copy(k, KV.at[0, 0], loc.at[2]),
        pltpu.make_async_copy(v, KV.at[1, 0], loc.at[3]),
        pltpu.make_async_copy(wq.at[:, cols(u, c)], W.at[pl.ds(0, 256)], loc.at[4]),
        pltpu.make_async_copy(wkv, WK, loc.at[5]),
    ]

    lane = lax.broadcasted_iota(jnp.int32, (1, 128), 1)
    r0, r1 = pos[0] // 64, pos[64] // 64
    s0, s1 = doc[0], doc[64]
    rows = [
        jnp.where((lane >= s0) & (lane <= r0), 0.0, NEG),
        jnp.where((lane >= s1) & (lane <= r1), 0.0, NEG),
        jnp.where(lane == r0, 1.0, 0.0),
        jnp.where(lane == r1, 1.0, 0.0),
        jnp.zeros((4, 128), F32),
    ]
    meta_val = jnp.concatenate(rows, axis=0)
    meta[...] = meta_val
    MQ[0] = meta_val
    MK[0] = meta_val
    jj = lax.broadcasted_iota(jnp.int32, (128, 256), 0)
    ii = lax.broadcasted_iota(jnp.int32, (128, 256), 1) % 128
    tri[...] = jnp.where((jj // 64 == ii // 64) & (jj > ii), NEG, 0.0)

    barrier = pltpu.get_barrier_semaphore()
    peers = [plane(d) for d in range(1, 8)] + [ring(d) for d in range(1, 8)]
    peers += [mate, far, far_mate, cross, cross_mate]
    for dev in peers:
        pl.semaphore_signal(barrier, inc=1, device_id=dev, device_id_type=MESH)
    for cp in own[:4]:
        cp.start()
    pl.semaphore_wait(barrier, len(peers))

    ORDER = (1, 7, 2, 6, 3, 5, 4)
    gk = {d: rc(k, KV.at[c, d], k_s.at[d], k_r.at[d], ring(d)) for d in ORDER}
    gv = {d: rc(v, KV.at[c, d], k_s.at[d], k_r.at[d], ring(d)) for d in ORDER}
    halves = (pl.ds(0, 64), pl.ds(64, 64))
    gk[4] = rc(KV.at[c, 3, halves[0]], KV.at[c, 4, halves[0]], k_s.at[4], k_r.at[4], ring(1))
    gk[0] = rc(KV.at[c, 5, halves[1]], KV.at[c, 4, halves[1]], k_s.at[0], k_r.at[0], ring(-1))
    gkv = {d: rc(KV.at[c, d], KV.at[c, d], v_s.at[d], v_r.at[d], mate) for d in ORDER}
    gmk = {d: rc(meta, MK.at[d], mk_s.at[d], mk_r.at[d], ring(d)) for d in ORDER}
    gmq = {d: rc(meta, MQ.at[d], mq_s.at[d], mq_r.at[d], plane(d)) for d in ORDER}

    def qd(i, src, d, dev):
        sems = (q_s, q_r) if i == 0 else (d_s, d_r)
        return rc(src, QD.at[d, i], sems[0].at[d], sems[1].at[d], dev)

    gq = {
        1: (qd(0, q, 1, right), qd(1, do, 1, right)),
        3: (qd(0, q, 3, left), qd(1, do, 3, left)),
        4: (qd(0, q, 4, side), qd(1, do, 4, side)),
        2: (qd(0, QD.at[1, 0], 2, right), qd(1, QD.at[3, 1], 2, left)),
        5: (qd(0, QD.at[4, 0], 5, right), qd(1, QD.at[4, 1], 5, right)),
        7: (qd(0, QD.at[4, 0], 7, left), qd(1, QD.at[4, 1], 7, left)),
        6: (qd(0, QD.at[2, 0], 6, side), qd(1, QD.at[2, 1], 6, side)),
    }

    @pl.when(c == 0)
    def _():
        for d in ORDER[:6]:
            gk[d].start()

    @pl.when(c == 1)
    def _():
        for d in ORDER[:6]:
            gv[d].start()

    for d, i in ((1, 0), (3, 1), (4, 0), (1, 1), (3, 0), (4, 1)):
        gq[d][i].start()
    for d in ORDER:
        gmk[d].start()
        gmq[d].start()

    color = (z + 2 * x + 4 * yl) % 8
    up, down = ring(1), ring(-1)
    whole, upper, lower = pl.ds(512, 512), pl.ds(512, 256), pl.ds(768, 256)

    def sub(f, shift, base=0):
        return pl.ds(pl.multiple_of(base + f * 2048 + ((color + shift) % 8) * 256, 256), 256)

    over = []
    for f in range(2):
        at = [(2 * (1 - u) + cc) * 4096 for cc in (c, 1 - c)]
        into = sub(f, 4)
        over.append([
            rc(wq.at[:, sub(f, 4, at[0])], W.at[upper, into], cs.at[f, 0], cr.at[f, 0], cross),
            rc(wq.at[:, sub(f, 4, at[1])], W.at[lower, into], cs.at[f, 1], cr.at[f, 1], cross_mate),
        ])
    for cp in over[0] + over[1]:
        cp.start()

    def spread(f, i, part, shift, dev):
        at = sub(f, shift)
        return rc(W.at[part, at], W.at[part, at], fs.at[f, i], fr.at[f, i], dev)

    near = [
        [spread(f, i, whole, 0, dev) for i, dev in enumerate((right, left, up, down, side))]
        for f in range(2)
    ]
    next_near = [
        [spread(0, 5, whole, 2, down), spread(0, 6, whole, 6, up)],
        [
            spread(1, 5, upper, 1, side),
            spread(1, 6, upper, 7, side),
            spread(1, 7, lower, 1, left),
            spread(1, 8, lower, 7, right),
        ],
    ]

    def relay(step):
        f = step % 2
        if step < 2:
            for cp in over[f]:
                cp.wait_recv()
            for cp in near[f]:
                cp.start()
        else:
            for i in ((0, 1), (2, 3))[f]:
                near[f][i].wait_recv()
            for cp in next_near[f]:
                cp.start()

    wpush = [rc(wq.at[:, cols(u, 1 - c)], W.at[pl.ds(256, 256)], w_s, w_r, mate)]
    for cp in wpush:
        cp.start()
    for cp in own[4:]:
        cp.start()

    def runs(ref, d, row):
        a = jnp.broadcast_to(ref[d, row : row + 1, :], (64, 128))
        b = jnp.broadcast_to(ref[d, row + 1 : row + 2, :], (64, 128))
        return jnp.concatenate([a, b], axis=0).astype(BF)

    def pass_on(*which):
        for d in which:
            gk[d].wait_recv()
            gkv[d].start()

    pass_on(1, 7)
    gq[1][0].wait_recv()
    gq[2][0].start()
    gq[3][1].wait_recv()
    gq[2][1].start()
    gq[4][0].wait_recv()
    gq[5][0].start()
    gq[7][0].start()
    pass_on(2, 6)
    gq[4][1].wait_recv()
    gq[5][1].start()
    gq[7][1].start()
    gq[1][1].wait_recv()
    gq[3][0].wait_recv()
    gk[3].wait_recv()
    gk[4].start()
    gkv[3].start()
    gk[5].wait_recv()
    gk[0].start()
    gkv[5].start()
    for i in range(2):
        gq[2][i].wait_recv()
        gq[6][i].start()
    relay(0)
    gk[0].wait_recv()
    pass_on(4)
    for cp in own[:4]:
        cp.wait()
    for d in (0,) + ORDER:
        if d:
            gmk[d].wait_recv()
            gkv[d].wait_recv()
        at = pl.ds(d * 128, 128)
        OH[at, :] = runs(MK, d, 2)
        KT[:, d * 128 : (d + 1) * 128] = KV[0, d].astype(F32).T.astype(BF)
    for d in ORDER:
        gmq[d].wait_recv()

    def rows_of(i, n):
        return KV[i, 2 * n : 2 * n + 2].reshape(256, 128)

    def stacked(i, d):
        return jnp.concatenate([QD[d, i, :, 0:128], QD[d, i, :, 128:256]], axis=0)

    def fold(val, op):
        return op(val.reshape(32, 8, 256), axis=0)

    def slot(g, dx):
        return (x - dx + 4) % 4, ((yl + g) % 2) * 4 + dx

    def first(g, j, carry):
        owner, d = slot(g, j + (j // 2) * (5 - 2 * j))

        @pl.when(d >= 5)
        def _():
            qd(0, q, d, right).wait_recv()
            qd(1, do, d, right).wait_recv()

        bias = runs(MQ, d, 0)
        qa = jnp.concatenate(
            [stacked(0, d), jnp.concatenate([bias, bias], axis=0)], axis=1
        )
        dd = stacked(1, d)
        own_tile = jnp.where(d == 0, 1.0, 0.0)
        top = jnp.full((8, 256), -3e38, F32)
        for n in range(4):
            at = pl.ds(n * 256, 256)
            s = mm(jnp.concatenate([rows_of(0, n), OH[at, :]], axis=1), qa, NT)
            if n == 0:
                s = jnp.concatenate([s[0:128] + tri[...] * own_tile, s[128:256]], axis=0)
            S[d, at, :] = s
            top = jnp.maximum(top, fold(s, jnp.max))
            DP[d, at, :] = mm(rows_of(1, n), dd, NT)
        m = jnp.max(top, axis=0, keepdims=True)
        mc = m * (INV * LOG2E)
        total = jnp.zeros((8, 256), F32)
        mixed = jnp.zeros((8, 256), F32)
        for n in range(4):
            at = pl.ds(n * 256, 256)
            e = jnp.exp2(S[d, at, :] * (INV * LOG2E) - mc)
            S[d, at, :] = e
            total = total + fold(e, jnp.sum)
            mixed = mixed + fold(e * DP[d, at, :], jnp.sum)
        total = jnp.sum(total, axis=0, keepdims=True)
        mixed = jnp.sum(mixed, axis=0, keepdims=True)
        mloc[g, pl.ds(owner, 1), :] = m * INV
        stat[g, pl.ds(owner, 1), :] = m * INV + jnp.log(total)
        stat[g, pl.ds(owner + 4, 1), :] = mixed / total
        return carry

    gs = [
        {d: rc(stat.at[g], stat_all.at[d, g], st_s.at[d, g], st_r.at[d, g], plane(d)) for d in ORDER}
        for g in range(2)
    ]
    for g in range(2):
        lax.fori_loop(0, 2, functools.partial(first, g), 0)
        if g == 0:
            relay(1)
        lax.fori_loop(2, 4, functools.partial(first, g), 0)
        for d in ORDER:
            gs[g][d].start()
    relay(2)

    def merge(g):
        parts = [stat[g]]
        for d in range(1, 8):
            gs[g][d].wait_recv()
            parts.append(stat_all[d, g])
        big = parts[0][0:4]
        for a in parts[1:]:
            big = jnp.maximum(big, a[0:4])
        tot = jnp.zeros((4, 256), F32)
        mix = jnp.zeros((4, 256), F32)
        for a in parts:
            w = jnp.exp(a[0:4] - big)
            tot = tot + w
            mix = mix + w * a[4:8]
        coef[g, 0:4, :] = jnp.exp(mloc[g] - (big + jnp.log(tot)))
        coef[g, 4:8, :] = mix / tot

    dk[...] = jnp.zeros_like(dk)
    dv[...] = jnp.zeros_like(dv)

    def second(g, j, carry):
        owner, d = slot(g, (2 - j) * (1 - j // 2) + (9 - 3 * j) * (j // 2))
        f = coef[g, pl.ds(owner, 1), :]
        delta = coef[g, pl.ds(owner + 4, 1), :]
        qq = stacked(0, d)
        dd = stacked(1, d)
        dqt = jnp.zeros((128, 256), F32)
        for n in range(4):
            at = pl.ds(n * 256, 256)
            pn = S[d, at, :] * f
            ds = (pn * (DP[d, at, :] - delta)).astype(BF)
            dv[at, :] += mm(pn.astype(BF), dd)
            dk[at, :] += mm(ds, qq)
            dqt = dqt + mm(KT[:, n * 256 : (n + 1) * 256], ds)
        dqs[d] = dqt.T.astype(BF)

        @pl.when(d > 0)
        def _():
            rc(dqs.at[d], dqr.at[d], dq_s.at[d], dq_r.at[d], owner_of(d)).start()

        return carry

    for g in range(2):
        merge(g)
        lax.fori_loop(0, 4, functools.partial(second, g), 0)

    first_core = c == 0
    pair_s[...] = jnp.where(first_core, dv[...], dk[...]).astype(BF)
    pair = rc(pair_s, pair_r, pr_s, pr_r, mate)
    pair.start()

    pair.wait_recv()
    for d in range(8):
        at = pl.ds(d * 128, 128)
        zs[d] = (jnp.where(first_core, dk[at, :], dv[at, :]) + pair_r[at, :].astype(F32)).astype(BF)
    relay(3)
    gz = {d: rc(zs.at[d], zr.at[d], z_s.at[d], z_r.at[d], ring(-d)) for d in ORDER}
    for d in ORDER:
        gz[d].start()

    dqsum = dqs[0].astype(F32)
    for d in range(1, 8):
        rc(dqs.at[d], dqr.at[d], dq_s.at[d], dq_r.at[d], owner_of(d)).wait_recv()
        dqsum = dqsum + dqr[d].astype(F32)
    dqsum = (dqsum * INV).astype(BF)
    dqf[:, 0:128] = dqsum[0:128]
    dqf[:, 128:256] = dqsum[128:256]
    gx = [
        rc(dqf, dqx.at[i], x_s.at[i], x_r.at[i], dev)
        for i, dev in enumerate((mate, far, far_mate))
    ]
    for cp in (gx[2], gx[1], gx[0]):
        cp.start()

    ksum = zs[0].astype(F32)
    for d in range(1, 8):
        gz[d].wait_recv()
        ksum = ksum + zr[d].astype(F32)
    hs[...] = ksum.astype(BF)
    gh = [
        rc(hs, hr.at[i], h_s.at[i], h_r.at[i], dev)
        for i, dev in enumerate((mate, far, far_mate))
    ]
    for cp in gh:
        cp.start()
    for cp in wpush:
        cp.wait_recv()
    for cp in own[4:]:
        cp.wait()
    for cp in near[0][2:] + near[1][:2] + near[1][4:] + next_near[0] + next_near[1]:
        cp.wait_recv()
    for cp in gx:
        cp.wait_recv()
    all_dq = jnp.concatenate([dqf[...], dqx[0], dqx[1], dqx[2]], axis=1)

    def query_part(n, carry):
        col = pl.ds(pl.multiple_of(n * 512, 512), 512)
        acc[:, col] = mm(all_dq, W[:, col])
        return carry

    lax.fori_loop(0, 8, query_part, 0)

    for cp in gh:
        cp.wait_recv()
    mine = hs[...].astype(F32) + hr[1].astype(F32)
    others = hr[0].astype(F32) + hr[2].astype(F32)
    dk_all = (jnp.where(first_core, mine, others) * INV).astype(BF)
    dv_all = jnp.where(first_core, others, mine).astype(BF)
    kvg = jnp.concatenate([dk_all, dv_all], axis=1)

    def finish(n, carry):
        col = pl.ds(pl.multiple_of(n * 512, 512), 512)
        out[:, col] = (acc[:, col] + mm(kvg, WK[:, col])).astype(BF)
        return carry

    lax.fori_loop(0, 8, finish, 0)

    for d in ORDER:
        for g in (gk, gkv, gmk, gmq, gs[0], gs[1], gz):
            g[d].wait_send()
        for cp in gq[d]:
            cp.wait_send()
        rc(dqs.at[d], dqr.at[d], dq_s.at[d], dq_r.at[d], owner_of(d)).wait_send()
    for cp in wpush + gx + gh + [pair, gk[0]]:
        cp.wait_send()
    for cp in over[0] + over[1] + near[0] + near[1] + next_near[0] + next_near[1]:
        cp.wait_send()


def on_device(queries, keys, values, dout, positions, doc_ids, w_query, w_kv):
    anys = pl.BlockSpec(memory_space=pl.ANY)
    smem = pl.BlockSpec(memory_space=pltpu.SMEM)
    V = pltpu.VMEM
    dma = pltpu.SemaphoreType.DMA
    scratch = [
        V((8, 2, 128, 256), BF), V((2, 8, 128, 128), BF), V((1024, 128), BF),
        V((128, 1024), BF), V((8, 8, 128), F32), V((8, 8, 128), F32), V((8, 128), F32),
        V((128, 256), F32), V((8, 1024, 256), F32), V((8, 1024, 256), F32),
        V((2, 8, 256), F32), V((2, 4, 256), F32), V((8, 2, 8, 256), F32), V((2, 8, 256), F32),
        V((1024, 128), F32), V((1024, 128), F32), V((8, 256, 128), BF), V((8, 256, 128), BF),
        V((1024, 128), BF), V((1024, 128), BF), V((8, 128, 128), BF), V((8, 128, 128), BF),
        V((128, 128), BF), V((3, 128, 128), BF), V((128, 256), BF), V((3, 128, 256), BF),
        V((1024, 4096), BF), V((256, 4096), BF), V((128, 4096), F32),
    ]
    scratch += [dma((8,))] * 12 + [dma((8, 2))] * 2 + [dma((8,))] * 4
    scratch += [dma, dma, dma((3,)), dma((3,)), dma((3,)), dma((3,)), dma, dma]
    scratch += [dma((2, 2)), dma((2, 2)), dma((2, 9)), dma((2, 9)), dma((6,))]
    return pl.pallas_call(
        kernel,
        out_shape=pltpu.VMEM((128, 4096), BF),
        in_specs=[smem, smem] + [anys] * 6,
        out_specs=pl.BlockSpec(memory_space=pltpu.VMEM),
        scratch_shapes=scratch,
        compiler_params=pltpu.CompilerParams(
            collective_id=0, has_side_effects=True, vmem_limit_bytes=60 * 1024 * 1024
        ),
    )(positions, doc_ids, queries, dout, keys, values, w_query, w_kv)


def solution(mesh):
    torus = Mesh(mesh.devices.reshape(8, 2, 4, 2, 2), CTX + HEAD)
    return jax.shard_map(
        on_device,
        mesh=torus,
        in_specs=(
            P(CTX, HEAD),
            P(CTX, None),
            P(CTX, None),
            P(CTX, HEAD),
            P(CTX),
            P(CTX),
            P(HEAD, None),
            P(None, HEAD),
        ),
        out_specs=P(CTX, HEAD),
        check_vma=False,
    )
```

```python
import functools
import math

import jax
import jax.numpy as jnp
from jax import lax
from jax.experimental import pallas as pl
from jax.experimental.pallas import tpu as pltpu
from jax.sharding import Mesh
from jax.sharding import PartitionSpec as P

CTX = ("z", "yl", "x")
HEAD = ("u", "c")
MESH = pl.DeviceIdType.MESH
BF = jnp.bfloat16
F32 = jnp.float32
NEG = -1e30
INV = 1.0 / math.sqrt(128)
LOG2E = 1.4426950408889634
NT = (((1,), (1,)), ((), ()))
NN = (((1,), (0,)), ((), ()))


def mm(a, b, dims=NN):
    return lax.dot_general(a, b, dims, preferred_element_type=F32)


def kernel(
    pos, doc, q, do, k, v, wq, wkv, out,
    QD, KV, OH, KT, MQ, MK, meta, tri, S, DP, stat, mloc, stat_all, coef,
    dk, dv, dqs, dqr, pair_s, pair_r, zs, zr, hs, hr, dqf, dqx, W, WK, acc,
    q_s, q_r, d_s, d_r, k_s, k_r, v_s, v_r, mq_s, mq_r, mk_s, mk_r, st_s, st_r,
    dq_s, dq_r, z_s, z_r, pr_s, pr_r, h_s, h_r, x_s, x_r, w_s, w_r, cs, cr, fs, fr, loc,
):
    z, yl, x = lax.axis_index("z"), lax.axis_index("yl"), lax.axis_index("x")
    u, c = lax.axis_index("u"), lax.axis_index("c")

    def plane(d):
        return (z, (yl + d // 4) % 2, (x + d % 4) % 4, u, c)

    def owner_of(d):
        return (z, (yl + d // 4) % 2, (x + 4 - d % 4) % 4, u, c)

    def ring(d):
        return ((z + d + 8) % 8, yl, x, u, c)

    mate = (z, yl, x, u, 1 - c)
    side = (z, 1 - yl, x, u, c)
    left, right = (z, yl, (x + 3) % 4, u, c), (z, yl, (x + 1) % 4, u, c)
    far = (z, yl, x, 1 - u, c)
    far_mate = (z, yl, x, 1 - u, 1 - c)
    cross = (z, 1 - yl, x, 1 - u, c)
    cross_mate = (z, 1 - yl, x, 1 - u, 1 - c)

    def rc(src, dst, ss, rs, dev):
        return pltpu.make_async_remote_copy(
            src_ref=src, dst_ref=dst, send_sem=ss, recv_sem=rs, device_id=dev, device_id_type=MESH
        )

    def cols(uu, cc):
        return pl.ds(pl.multiple_of((2 * uu + cc) * 4096, 4096), 4096)

    own = [
        pltpu.make_async_copy(q, QD.at[0, 0], loc.at[0]),
        pltpu.make_async_copy(do, QD.at[0, 1], loc.at[1]),
        pltpu.make_async_copy(k, KV.at[0, 0], loc.at[2]),
        pltpu.make_async_copy(v, KV.at[1, 0], loc.at[3]),
        pltpu.make_async_copy(wq.at[:, cols(u, c)], W.at[pl.ds(0, 256)], loc.at[4]),
        pltpu.make_async_copy(wkv, WK, loc.at[5]),
    ]

    lane = lax.broadcasted_iota(jnp.int32, (1, 128), 1)
    r0, r1 = pos[0] // 64, pos[64] // 64
    s0, s1 = doc[0], doc[64]
    rows = [
        jnp.where((lane >= s0) & (lane <= r0), 0.0, NEG),
        jnp.where((lane >= s1) & (lane <= r1), 0.0, NEG),
        jnp.where(lane == r0, 1.0, 0.0),
        jnp.where(lane == r1, 1.0, 0.0),
        jnp.zeros((4, 128), F32),
    ]
    meta_val = jnp.concatenate(rows, axis=0)
    meta[...] = meta_val
    MQ[0] = meta_val
    MK[0] = meta_val
    jj = lax.broadcasted_iota(jnp.int32, (128, 256), 0)
    ii = lax.broadcasted_iota(jnp.int32, (128, 256), 1) % 128
    tri[...] = jnp.where((jj // 64 == ii // 64) & (jj > ii), NEG, 0.0)

    barrier = pltpu.get_barrier_semaphore()
    peers = [plane(d) for d in range(1, 8)] + [ring(d) for d in range(1, 8)]
    peers += [mate, far, far_mate, cross, cross_mate]
    for dev in peers:
        pl.semaphore_signal(barrier, inc=1, device_id=dev, device_id_type=MESH)
    for cp in own[:4]:
        cp.start()
    pl.semaphore_wait(barrier, len(peers))

    ORDER = (1, 7, 2, 6, 3, 5, 4)
    gk = {d: rc(k, KV.at[c, d], k_s.at[d], k_r.at[d], ring(d)) for d in ORDER}
    gv = {d: rc(v, KV.at[c, d], k_s.at[d], k_r.at[d], ring(d)) for d in ORDER}
    halves = (pl.ds(0, 64), pl.ds(64, 64))
    gk[4] = rc(KV.at[c, 3, halves[0]], KV.at[c, 4, halves[0]], k_s.at[4], k_r.at[4], ring(1))
    gk[0] = rc(KV.at[c, 5, halves[1]], KV.at[c, 4, halves[1]], k_s.at[0], k_r.at[0], ring(-1))
    gkv = {d: rc(KV.at[c, d], KV.at[c, d], v_s.at[d], v_r.at[d], mate) for d in ORDER}
    gmk = {d: rc(meta, MK.at[d], mk_s.at[d], mk_r.at[d], ring(d)) for d in ORDER}
    gmq = {d: rc(meta, MQ.at[d], mq_s.at[d], mq_r.at[d], plane(d)) for d in ORDER}

    def qd(i, src, d, dev):
        sems = (q_s, q_r) if i == 0 else (d_s, d_r)
        return rc(src, QD.at[d, i], sems[0].at[d], sems[1].at[d], dev)

    gq = {
        1: (qd(0, q, 1, right), qd(1, do, 1, right)),
        3: (qd(0, q, 3, left), qd(1, do, 3, left)),
        4: (qd(0, q, 4, side), qd(1, do, 4, side)),
        2: (qd(0, QD.at[1, 0], 2, right), qd(1, QD.at[3, 1], 2, left)),
        5: (qd(0, QD.at[4, 0], 5, right), qd(1, QD.at[4, 1], 5, right)),
        7: (qd(0, QD.at[4, 0], 7, left), qd(1, QD.at[4, 1], 7, left)),
        6: (qd(0, QD.at[2, 0], 6, side), qd(1, QD.at[2, 1], 6, side)),
    }

    @pl.when(c == 0)
    def _():
        for d in ORDER[:6]:
            gk[d].start()

    @pl.when(c == 1)
    def _():
        for d in ORDER[:6]:
            gv[d].start()

    for d, i in ((1, 0), (3, 1), (4, 0), (1, 1), (3, 0), (4, 1)):
        gq[d][i].start()
    for d in ORDER:
        gmk[d].start()
        gmq[d].start()

    color = (z + 2 * x + 4 * yl) % 8
    up, down = ring(1), ring(-1)
    whole, upper, lower = pl.ds(512, 512), pl.ds(512, 256), pl.ds(768, 256)

    def sub(f, shift, base=0):
        return pl.ds(pl.multiple_of(base + f * 2048 + ((color + shift) % 8) * 256, 256), 256)

    over = []
    for f in range(2):
        at = [(2 * (1 - u) + cc) * 4096 for cc in (c, 1 - c)]
        into = sub(f, 4)
        over.append([
            rc(wq.at[:, sub(f, 4, at[0])], W.at[upper, into], cs.at[f, 0], cr.at[f, 0], cross),
            rc(wq.at[:, sub(f, 4, at[1])], W.at[lower, into], cs.at[f, 1], cr.at[f, 1], cross_mate),
        ])
    for cp in over[0] + over[1]:
        cp.start()

    def spread(f, i, part, shift, dev):
        at = sub(f, shift)
        return rc(W.at[part, at], W.at[part, at], fs.at[f, i], fr.at[f, i], dev)

    near = [
        [spread(f, i, whole, 0, dev) for i, dev in enumerate((right, left, up, down, side))]
        for f in range(2)
    ]
    next_near = [
        [spread(0, 5, whole, 2, down), spread(0, 6, whole, 6, up)],
        [
            spread(1, 5, upper, 1, side),
            spread(1, 6, upper, 7, side),
            spread(1, 7, lower, 1, left),
            spread(1, 8, lower, 7, right),
        ],
    ]

    def relay(step):
        f = step % 2
        if step < 2:
            for cp in over[f]:
                cp.wait_recv()
            for cp in near[f]:
                cp.start()
        else:
            for i in ((0, 1), (2, 3))[f]:
                near[f][i].wait_recv()
            for cp in next_near[f]:
                cp.start()

    wpush = [rc(wq.at[:, cols(u, 1 - c)], W.at[pl.ds(256, 256)], w_s, w_r, mate)]
    for cp in own[4:]:
        cp.start()

    def runs(ref, d, row):
        a = jnp.broadcast_to(ref[d, row : row + 1, :], (64, 128))
        b = jnp.broadcast_to(ref[d, row + 1 : row + 2, :], (64, 128))
        return jnp.concatenate([a, b], axis=0).astype(BF)

    def pass_on(*which):
        for d in which:
            gk[d].wait_recv()
            gkv[d].start()

    pass_on(1, 7)
    gq[1][0].wait_recv()
    gq[2][0].start()
    gq[3][1].wait_recv()
    gq[2][1].start()
    gq[4][0].wait_recv()
    gq[5][0].start()
    gq[7][0].start()
    pass_on(2, 6)
    gq[4][1].wait_recv()
    gq[5][1].start()
    gq[7][1].start()
    gq[1][1].wait_recv()
    gq[3][0].wait_recv()
    gk[3].wait_recv()
    gk[4].start()
    gkv[3].start()
    gk[5].wait_recv()
    gk[0].start()
    gkv[5].start()
    for i in range(2):
        gq[2][i].wait_recv()
        gq[6][i].start()
    relay(0)
    gk[0].wait_recv()
    pass_on(4)
    for cp in wpush:
        cp.start()
    for cp in own[:4]:
        cp.wait()
    for d in (0,) + ORDER:
        if d:
            gmk[d].wait_recv()
            gkv[d].wait_recv()
        at = pl.ds(d * 128, 128)
        OH[at, :] = runs(MK, d, 2)
    for d in ORDER:
        gmq[d].wait_recv()

    def rows_of(i, n):
        return KV[i, 2 * n : 2 * n + 2].reshape(256, 128)

    def stacked(i, d):
        return jnp.concatenate([QD[d, i, :, 0:128], QD[d, i, :, 128:256]], axis=0)

    def fold(val, op):
        return op(val.reshape(32, 8, 256), axis=0)

    def slot(g, dx):
        return (x - dx + 4) % 4, ((yl + g) % 2) * 4 + dx

    def first(g, j, carry):
        owner, d = slot(g, j + (j // 2) * (5 - 2 * j))

        @pl.when(d >= 5)
        def _():
            qd(0, q, d, right).wait_recv()
            qd(1, do, d, right).wait_recv()

        bias = runs(MQ, d, 0)
        qa = jnp.concatenate(
            [stacked(0, d), jnp.concatenate([bias, bias], axis=0)], axis=1
        )
        dd = stacked(1, d)
        own_tile = jnp.where(d == 0, 1.0, 0.0)
        top = jnp.full((8, 256), -3e38, F32)
        for n in range(4):
            at = pl.ds(n * 256, 256)
            s = mm(jnp.concatenate([rows_of(0, n), OH[at, :]], axis=1), qa, NT)
            if n == 0:
                s = jnp.concatenate([s[0:128] + tri[...] * own_tile, s[128:256]], axis=0)
            S[d, at, :] = s
            top = jnp.maximum(top, fold(s, jnp.max))
            DP[d, at, :] = mm(rows_of(1, n), dd, NT)
        m = jnp.max(top, axis=0, keepdims=True)
        mc = m * (INV * LOG2E)
        total = jnp.zeros((8, 256), F32)
        mixed = jnp.zeros((8, 256), F32)
        for n in range(4):
            at = pl.ds(n * 256, 256)
            e = jnp.exp2(S[d, at, :] * (INV * LOG2E) - mc)
            S[d, at, :] = e
            total = total + fold(e, jnp.sum)
            mixed = mixed + fold(e * DP[d, at, :], jnp.sum)
        total = jnp.sum(total, axis=0, keepdims=True)
        mixed = jnp.sum(mixed, axis=0, keepdims=True)
        mloc[g, pl.ds(owner, 1), :] = m * INV
        stat[g, pl.ds(owner, 1), :] = m * INV + jnp.log(total)
        stat[g, pl.ds(owner + 4, 1), :] = mixed / total
        return carry

    gs = [
        {d: rc(stat.at[g], stat_all.at[d, g], st_s.at[d, g], st_r.at[d, g], plane(d)) for d in ORDER}
        for g in range(2)
    ]
    for g in range(2):
        lax.fori_loop(0, 2, functools.partial(first, g), 0)
        if g == 0:
            relay(1)
        lax.fori_loop(2, 4, functools.partial(first, g), 0)
        for d in ORDER:
            gs[g][d].start()
    relay(2)

    def merge(g):
        parts = [stat[g]]
        for d in range(1, 8):
            gs[g][d].wait_recv()
            parts.append(stat_all[d, g])
        big = parts[0][0:4]
        for a in parts[1:]:
            big = jnp.maximum(big, a[0:4])
        tot = jnp.zeros((4, 256), F32)
        mix = jnp.zeros((4, 256), F32)
        for a in parts:
            w = jnp.exp(a[0:4] - big)
            tot = tot + w
            mix = mix + w * a[4:8]
        coef[g, 0:4, :] = jnp.exp(mloc[g] - (big + jnp.log(tot)))
        coef[g, 4:8, :] = mix / tot

    for d in range(8):
        KT[:, d * 128 : (d + 1) * 128] = KV[0, d].astype(F32).T.astype(BF)
    dk[...] = jnp.zeros_like(dk)
    dv[...] = jnp.zeros_like(dv)

    def second(g, j, carry):
        owner, d = slot(g, (2 - j) * (1 - j // 2) + (9 - 3 * j) * (j // 2))
        f = coef[g, pl.ds(owner, 1), :]
        delta = coef[g, pl.ds(owner + 4, 1), :]
        qq = stacked(0, d)
        dd = stacked(1, d)
        dqt = jnp.zeros((128, 256), F32)
        for n in range(4):
            at = pl.ds(n * 256, 256)
            pn = S[d, at, :] * f
            ds = (pn * (DP[d, at, :] - delta)).astype(BF)
            dv[at, :] += mm(pn.astype(BF), dd)
            dk[at, :] += mm(ds, qq)
            dqt = dqt + mm(KT[:, n * 256 : (n + 1) * 256], ds)
        dqs[d] = dqt.T.astype(BF)

        @pl.when(d > 0)
        def _():
            rc(dqs.at[d], dqr.at[d], dq_s.at[d], dq_r.at[d], owner_of(d)).start()

        return carry

    for g in range(2):
        merge(g)
        lax.fori_loop(0, 4, functools.partial(second, g), 0)

    first_core = c == 0
    pair_s[...] = jnp.where(first_core, dv[...], dk[...]).astype(BF)
    pair = rc(pair_s, pair_r, pr_s, pr_r, mate)
    pair.start()

    pair.wait_recv()
    for d in range(8):
        at = pl.ds(d * 128, 128)
        zs[d] = (jnp.where(first_core, dk[at, :], dv[at, :]) + pair_r[at, :].astype(F32)).astype(BF)
    relay(3)
    gz = {d: rc(zs.at[d], zr.at[d], z_s.at[d], z_r.at[d], ring(-d)) for d in ORDER}
    for d in ORDER:
        gz[d].start()

    dqsum = dqs[0].astype(F32)
    for d in range(1, 8):
        rc(dqs.at[d], dqr.at[d], dq_s.at[d], dq_r.at[d], owner_of(d)).wait_recv()
        dqsum = dqsum + dqr[d].astype(F32)
    dqsum = (dqsum * INV).astype(BF)
    dqf[:, 0:128] = dqsum[0:128]
    dqf[:, 128:256] = dqsum[128:256]
    gx = [
        rc(dqf, dqx.at[i], x_s.at[i], x_r.at[i], dev)
        for i, dev in enumerate((mate, far, far_mate))
    ]
    for cp in (gx[2], gx[1], gx[0]):
        cp.start()

    ksum = zs[0].astype(F32)
    for d in range(1, 8):
        gz[d].wait_recv()
        ksum = ksum + zr[d].astype(F32)
    hs[...] = ksum.astype(BF)
    gh = [
        rc(hs, hr.at[i], h_s.at[i], h_r.at[i], dev)
        for i, dev in enumerate((mate, far, far_mate))
    ]
    for cp in gh:
        cp.start()
    for cp in wpush:
        cp.wait_recv()
    for cp in own[4:]:
        cp.wait()
    for cp in gx:
        cp.wait_recv()
    all_dq = jnp.concatenate([dqf[...], dqx[0], dqx[1], dqx[2]], axis=1)

    def query_part(f, shifts):
        for shift in shifts:
            acc[:, sub(f, shift)] = mm(all_dq, W[:, sub(f, shift)])

    for cp in near[0][2:]:
        cp.wait_recv()
    query_part(0, (0, 1, 2, 4, 6, 7))
    for cp in near[1][:2] + near[1][4:]:
        cp.wait_recv()
    query_part(1, (0, 1, 2, 4, 6, 7))
    for f in range(2):
        for cp in next_near[f]:
            cp.wait_recv()
        query_part(f, (3, 5))

    for cp in gh:
        cp.wait_recv()
    mine = hs[...].astype(F32) + hr[1].astype(F32)
    others = hr[0].astype(F32) + hr[2].astype(F32)
    dk_all = (jnp.where(first_core, mine, others) * INV).astype(BF)
    dv_all = jnp.where(first_core, others, mine).astype(BF)
    kvg = jnp.concatenate([dk_all, dv_all], axis=1)

    def finish(n, carry):
        col = pl.ds(pl.multiple_of(n * 512, 512), 512)
        out[:, col] = (acc[:, col] + mm(kvg, WK[:, col])).astype(BF)
        return carry

    lax.fori_loop(0, 8, finish, 0, unroll=2)

    for d in ORDER:
        for g in (gk, gkv, gmk, gmq, gs[0], gs[1], gz):
            g[d].wait_send()
        for cp in gq[d]:
            cp.wait_send()
        rc(dqs.at[d], dqr.at[d], dq_s.at[d], dq_r.at[d], owner_of(d)).wait_send()
    for cp in wpush + gx + gh + [pair, gk[0]]:
        cp.wait_send()
    for cp in over[0] + over[1] + near[0] + near[1] + next_near[0] + next_near[1]:
        cp.wait_send()


def on_device(queries, keys, values, dout, positions, doc_ids, w_query, w_kv):
    anys = pl.BlockSpec(memory_space=pl.ANY)
    smem = pl.BlockSpec(memory_space=pltpu.SMEM)
    V = pltpu.VMEM
    dma = pltpu.SemaphoreType.DMA
    scratch = [
        V((8, 2, 128, 256), BF), V((2, 8, 128, 128), BF), V((1024, 128), BF),
        V((128, 1024), BF), V((8, 8, 128), F32), V((8, 8, 128), F32), V((8, 128), F32),
        V((128, 256), F32), V((8, 1024, 256), F32), V((8, 1024, 256), F32),
        V((2, 8, 256), F32), V((2, 4, 256), F32), V((8, 2, 8, 256), F32), V((2, 8, 256), F32),
        V((1024, 128), F32), V((1024, 128), F32), V((8, 256, 128), BF), V((8, 256, 128), BF),
        V((1024, 128), BF), V((1024, 128), BF), V((8, 128, 128), BF), V((8, 128, 128), BF),
        V((128, 128), BF), V((3, 128, 128), BF), V((128, 256), BF), V((3, 128, 256), BF),
        V((1024, 4096), BF), V((256, 4096), BF), V((128, 4096), F32),
    ]
    scratch += [dma((8,))] * 12 + [dma((8, 2))] * 2 + [dma((8,))] * 4
    scratch += [dma, dma, dma((3,)), dma((3,)), dma((3,)), dma((3,)), dma, dma]
    scratch += [dma((2, 2)), dma((2, 2)), dma((2, 9)), dma((2, 9)), dma((6,))]
    return pl.pallas_call(
        kernel,
        out_shape=pltpu.VMEM((128, 4096), BF),
        in_specs=[smem, smem] + [anys] * 6,
        out_specs=pl.BlockSpec(memory_space=pltpu.VMEM),
        scratch_shapes=scratch,
        compiler_params=pltpu.CompilerParams(
            collective_id=0, has_side_effects=True, vmem_limit_bytes=60 * 1024 * 1024
        ),
    )(positions, doc_ids, queries, dout, keys, values, w_query, w_kv)


def solution(mesh):
    torus = Mesh(mesh.devices.reshape(8, 2, 4, 2, 2), CTX + HEAD)
    return jax.shard_map(
        on_device,
        mesh=torus,
        in_specs=(
            P(CTX, HEAD),
            P(CTX, None),
            P(CTX, None),
            P(CTX, HEAD),
            P(CTX),
            P(CTX),
            P(HEAD, None),
            P(None, HEAD),
        ),
        out_specs=P(CTX, HEAD),
        check_vma=False,
    )
```

```python
import functools
import math

import jax
import jax.numpy as jnp
from jax import lax
from jax.experimental import pallas as pl
from jax.experimental.pallas import tpu as pltpu
from jax.sharding import Mesh
from jax.sharding import PartitionSpec as P

CTX = ("z", "yl", "x")
HEAD = ("u", "c")
MESH = pl.DeviceIdType.MESH
BF = jnp.bfloat16
F32 = jnp.float32
NEG = -1e30
INV = 1.0 / math.sqrt(128)
LOG2E = 1.4426950408889634
NT = (((1,), (1,)), ((), ()))
NN = (((1,), (0,)), ((), ()))


def mm(a, b, dims=NN):
    return lax.dot_general(a, b, dims, preferred_element_type=F32)


def kernel(
    pos, doc, q, do, k, v, wq, wkv, out,
    QD, KV, OH, KT, MQ, MK, meta, tri, S, DP, stat, mloc, stat_all, coef,
    dk, dv, dqs, dqr, pair_s, pair_r, zs, zr, hs, hr, dqf, dqx, W, WK, acc,
    q_s, q_r, d_s, d_r, k_s, k_r, v_s, v_r, mq_s, mq_r, mk_s, mk_r, st_s, st_r,
    dq_s, dq_r, z_s, z_r, pr_s, pr_r, h_s, h_r, x_s, x_r, w_s, w_r, cs, cr, fs, fr, loc,
):
    z, yl, x = lax.axis_index("z"), lax.axis_index("yl"), lax.axis_index("x")
    u, c = lax.axis_index("u"), lax.axis_index("c")

    def plane(d):
        return (z, (yl + d // 4) % 2, (x + d % 4) % 4, u, c)

    def owner_of(d):
        return (z, (yl + d // 4) % 2, (x + 4 - d % 4) % 4, u, c)

    def ring(d):
        return ((z + d + 8) % 8, yl, x, u, c)

    mate = (z, yl, x, u, 1 - c)
    side = (z, 1 - yl, x, u, c)
    left, right = (z, yl, (x + 3) % 4, u, c), (z, yl, (x + 1) % 4, u, c)
    far = (z, yl, x, 1 - u, c)
    far_mate = (z, yl, x, 1 - u, 1 - c)
    cross = (z, 1 - yl, x, 1 - u, c)
    cross_mate = (z, 1 - yl, x, 1 - u, 1 - c)

    def rc(src, dst, ss, rs, dev):
        return pltpu.make_async_remote_copy(
            src_ref=src, dst_ref=dst, send_sem=ss, recv_sem=rs, device_id=dev, device_id_type=MESH
        )

    def cols(uu, cc):
        return pl.ds(pl.multiple_of((2 * uu + cc) * 4096, 4096), 4096)

    own = [
        pltpu.make_async_copy(q, QD.at[0, 0], loc.at[0]),
        pltpu.make_async_copy(do, QD.at[0, 1], loc.at[1]),
        pltpu.make_async_copy(k, KV.at[0, 0], loc.at[2]),
        pltpu.make_async_copy(v, KV.at[1, 0], loc.at[3]),
        pltpu.make_async_copy(wq.at[:, cols(u, c)], W.at[pl.ds(0, 256)], loc.at[4]),
        pltpu.make_async_copy(wkv, WK, loc.at[5]),
    ]

    lane = lax.broadcasted_iota(jnp.int32, (1, 128), 1)
    r0, r1 = pos[0] // 64, pos[64] // 64
    s0, s1 = doc[0], doc[64]
    rows = [
        jnp.where((lane >= s0) & (lane <= r0), 0.0, NEG),
        jnp.where((lane >= s1) & (lane <= r1), 0.0, NEG),
        jnp.where(lane == r0, 1.0, 0.0),
        jnp.where(lane == r1, 1.0, 0.0),
        jnp.zeros((4, 128), F32),
    ]
    meta_val = jnp.concatenate(rows, axis=0)
    meta[...] = meta_val
    MQ[0] = meta_val
    MK[0] = meta_val
    jj = lax.broadcasted_iota(jnp.int32, (128, 256), 0)
    ii = lax.broadcasted_iota(jnp.int32, (128, 256), 1) % 128
    tri[...] = jnp.where((jj // 64 == ii // 64) & (jj > ii), NEG, 0.0)

    barrier = pltpu.get_barrier_semaphore()
    peers = [plane(d) for d in range(1, 8)] + [ring(d) for d in range(1, 8)]
    peers += [mate, far, far_mate, cross, cross_mate]
    for dev in peers:
        pl.semaphore_signal(barrier, inc=1, device_id=dev, device_id_type=MESH)
    for cp in own[:4]:
        cp.start()
    pl.semaphore_wait(barrier, len(peers))

    ORDER = (1, 7, 2, 6, 3, 5, 4)
    gk = {d: rc(k, KV.at[c, d], k_s.at[d], k_r.at[d], ring(d)) for d in ORDER}
    gv = {d: rc(v, KV.at[c, d], k_s.at[d], k_r.at[d], ring(d)) for d in ORDER}
    halves = (pl.ds(0, 64), pl.ds(64, 64))
    gk[4] = rc(KV.at[c, 3, halves[0]], KV.at[c, 4, halves[0]], k_s.at[4], k_r.at[4], ring(1))
    gk[0] = rc(KV.at[c, 5, halves[1]], KV.at[c, 4, halves[1]], k_s.at[0], k_r.at[0], ring(-1))
    gkv = {d: rc(KV.at[c, d], KV.at[c, d], v_s.at[d], v_r.at[d], mate) for d in ORDER}
    gmk = {d: rc(meta, MK.at[d], mk_s.at[d], mk_r.at[d], ring(d)) for d in ORDER}
    gmq = {d: rc(meta, MQ.at[d], mq_s.at[d], mq_r.at[d], plane(d)) for d in ORDER}

    def qd(i, src, d, dev):
        sems = (q_s, q_r) if i == 0 else (d_s, d_r)
        return rc(src, QD.at[d, i], sems[0].at[d], sems[1].at[d], dev)

    gq = {
        1: (qd(0, q, 1, right), qd(1, do, 1, right)),
        3: (qd(0, q, 3, left), qd(1, do, 3, left)),
        4: (qd(0, q, 4, side), qd(1, do, 4, side)),
        2: (qd(0, QD.at[1, 0], 2, right), qd(1, QD.at[3, 1], 2, left)),
        5: (qd(0, QD.at[4, 0], 5, right), qd(1, QD.at[4, 1], 5, right)),
        7: (qd(0, QD.at[4, 0], 7, left), qd(1, QD.at[4, 1], 7, left)),
        6: (qd(0, QD.at[2, 0], 6, side), qd(1, QD.at[2, 1], 6, side)),
    }

    @pl.when(c == 0)
    def _():
        for d in ORDER[:6]:
            gk[d].start()

    @pl.when(c == 1)
    def _():
        for d in ORDER[:6]:
            gv[d].start()

    for d, i in ((1, 0), (3, 1), (4, 0), (1, 1), (3, 0), (4, 1)):
        gq[d][i].start()
    for d in ORDER:
        gmk[d].start()
        gmq[d].start()

    color = (z + 2 * x + 4 * yl) % 8
    up, down = ring(1), ring(-1)
    whole, upper, lower = pl.ds(512, 512), pl.ds(512, 256), pl.ds(768, 256)

    def sub(f, shift, base=0):
        return pl.ds(pl.multiple_of(base + f * 2048 + ((color + shift) % 8) * 256, 256), 256)

    over = []
    for f in range(2):
        at = [(2 * (1 - u) + cc) * 4096 for cc in (c, 1 - c)]
        into = sub(f, 4)
        over.append([
            rc(wq.at[:, sub(f, 4, at[0])], W.at[upper, into], cs.at[f, 0], cr.at[f, 0], cross),
            rc(wq.at[:, sub(f, 4, at[1])], W.at[lower, into], cs.at[f, 1], cr.at[f, 1], cross_mate),
        ])
    for cp in over[0] + over[1]:
        cp.start()

    def spread(f, i, part, shift, dev):
        at = sub(f, shift)
        return rc(W.at[part, at], W.at[part, at], fs.at[f, i], fr.at[f, i], dev)

    near = [
        [spread(f, i, whole, 0, dev) for i, dev in enumerate((right, left, up, down, side))]
        for f in range(2)
    ]
    next_near = [
        [spread(0, 5, whole, 2, down), spread(0, 6, whole, 6, up)],
        [
            spread(1, 5, whole, 1, left),
            spread(1, 6, whole, 7, right),
        ],
    ]

    def relay(step):
        f = step % 2
        if step < 2:
            for cp in over[f]:
                cp.wait_recv()
            for cp in near[f]:
                cp.start()
        else:
            for i in ((0, 1), (2, 3))[f]:
                near[f][i].wait_recv()
            for cp in next_near[f]:
                cp.start()

    wpush = [rc(wq.at[:, cols(u, 1 - c)], W.at[pl.ds(256, 256)], w_s, w_r, mate)]
    for cp in own[4:]:
        cp.start()

    def runs(ref, d, row):
        a = jnp.broadcast_to(ref[d, row : row + 1, :], (64, 128))
        b = jnp.broadcast_to(ref[d, row + 1 : row + 2, :], (64, 128))
        return jnp.concatenate([a, b], axis=0).astype(BF)

    def pass_on(*which):
        for d in which:
            gk[d].wait_recv()
            gkv[d].start()

    pass_on(1, 7)
    gq[1][0].wait_recv()
    gq[2][0].start()
    gq[3][1].wait_recv()
    gq[2][1].start()
    gq[4][0].wait_recv()
    gq[5][0].start()
    gq[7][0].start()
    pass_on(2, 6)
    gq[4][1].wait_recv()
    gq[5][1].start()
    gq[7][1].start()
    gq[1][1].wait_recv()
    gq[3][0].wait_recv()
    gk[3].wait_recv()
    gk[4].start()
    gkv[3].start()
    gk[5].wait_recv()
    gk[0].start()
    gkv[5].start()
    for i in range(2):
        gq[2][i].wait_recv()
        gq[6][i].start()
    relay(0)
    gk[0].wait_recv()
    pass_on(4)
    for cp in wpush:
        cp.start()
    for cp in own[:4]:
        cp.wait()
    for d in (0,) + ORDER:
        if d:
            gmk[d].wait_recv()
            gkv[d].wait_recv()
        at = pl.ds(d * 128, 128)
        OH[at, :] = runs(MK, d, 2)
    for d in ORDER:
        gmq[d].wait_recv()

    def rows_of(i, n):
        return KV[i, 2 * n : 2 * n + 2].reshape(256, 128)

    def stacked(i, d):
        return jnp.concatenate([QD[d, i, :, 0:128], QD[d, i, :, 128:256]], axis=0)

    def fold(val, op):
        return op(val.reshape(32, 8, 256), axis=0)

    def slot(g, dx):
        return (x - dx + 4) % 4, ((yl + g) % 2) * 4 + dx

    def first(g, j, carry):
        owner, d = slot(g, j + (j // 2) * (5 - 2 * j))

        @pl.when(d >= 5)
        def _():
            qd(0, q, d, right).wait_recv()
            qd(1, do, d, right).wait_recv()

        bias = runs(MQ, d, 0)
        qa = jnp.concatenate(
            [stacked(0, d), jnp.concatenate([bias, bias], axis=0)], axis=1
        )
        dd = stacked(1, d)
        own_tile = jnp.where(d == 0, 1.0, 0.0)
        top = jnp.full((8, 256), -3e38, F32)
        for n in range(4):
            at = pl.ds(n * 256, 256)
            s = mm(jnp.concatenate([rows_of(0, n), OH[at, :]], axis=1), qa, NT)
            if n == 0:
                s = jnp.concatenate([s[0:128] + tri[...] * own_tile, s[128:256]], axis=0)
            S[d, at, :] = s
            top = jnp.maximum(top, fold(s, jnp.max))
            DP[d, at, :] = mm(rows_of(1, n), dd, NT)
        m = jnp.max(top, axis=0, keepdims=True)
        mc = m * (INV * LOG2E)
        total = jnp.zeros((8, 256), F32)
        mixed = jnp.zeros((8, 256), F32)
        for n in range(4):
            at = pl.ds(n * 256, 256)
            e = jnp.exp2(S[d, at, :] * (INV * LOG2E) - mc)
            S[d, at, :] = e
            total = total + fold(e, jnp.sum)
            mixed = mixed + fold(e * DP[d, at, :], jnp.sum)
        total = jnp.sum(total, axis=0, keepdims=True)
        mixed = jnp.sum(mixed, axis=0, keepdims=True)
        mloc[g, pl.ds(owner, 1), :] = m * INV
        stat[g, pl.ds(owner, 1), :] = m * INV + jnp.log(total)
        stat[g, pl.ds(owner + 4, 1), :] = mixed / total
        return carry

    gs = [
        {d: rc(stat.at[g], stat_all.at[d, g], st_s.at[d, g], st_r.at[d, g], plane(d)) for d in ORDER}
        for g in range(2)
    ]
    for g in range(2):
        lax.fori_loop(0, 1, functools.partial(first, g), 0)
        relay(1 + g)
        lax.fori_loop(1, 4, functools.partial(first, g), 0)
        for d in ORDER:
            gs[g][d].start()

    def merge(g):
        parts = [stat[g]]
        for d in range(1, 8):
            gs[g][d].wait_recv()
            parts.append(stat_all[d, g])
        big = parts[0][0:4]
        for a in parts[1:]:
            big = jnp.maximum(big, a[0:4])
        tot = jnp.zeros((4, 256), F32)
        mix = jnp.zeros((4, 256), F32)
        for a in parts:
            w = jnp.exp(a[0:4] - big)
            tot = tot + w
            mix = mix + w * a[4:8]
        coef[g, 0:4, :] = jnp.exp(mloc[g] - (big + jnp.log(tot)))
        coef[g, 4:8, :] = mix / tot

    for d in range(8):
        KT[:, d * 128 : (d + 1) * 128] = KV[0, d].astype(F32).T.astype(BF)
    dk[...] = jnp.zeros_like(dk)
    dv[...] = jnp.zeros_like(dv)

    def second(g, j, carry):
        owner, d = slot(g, (2 - j) * (1 - j // 2) + (9 - 3 * j) * (j // 2))
        f = coef[g, pl.ds(owner, 1), :]
        delta = coef[g, pl.ds(owner + 4, 1), :]
        qq = stacked(0, d)
        dd = stacked(1, d)
        dqt = jnp.zeros((128, 256), F32)
        for n in range(4):
            at = pl.ds(n * 256, 256)
            pn = S[d, at, :] * f
            ds = (pn * (DP[d, at, :] - delta)).astype(BF)
            dv[at, :] += mm(pn.astype(BF), dd)
            dk[at, :] += mm(ds, qq)
            dqt = dqt + mm(KT[:, n * 256 : (n + 1) * 256], ds)
        dqs[d] = dqt.T.astype(BF)

        @pl.when(d > 0)
        def _():
            rc(dqs.at[d], dqr.at[d], dq_s.at[d], dq_r.at[d], owner_of(d)).start()

        return carry

    for g in range(2):
        merge(g)
        lax.fori_loop(0, 4, functools.partial(second, g), 0)

    first_core = c == 0
    pair_s[...] = jnp.where(first_core, dv[...], dk[...]).astype(BF)
    pair = rc(pair_s, pair_r, pr_s, pr_r, mate)
    pair.start()

    pair.wait_recv()
    for d in range(8):
        at = pl.ds(d * 128, 128)
        zs[d] = (jnp.where(first_core, dk[at, :], dv[at, :]) + pair_r[at, :].astype(F32)).astype(BF)
    relay(3)
    gz = {d: rc(zs.at[d], zr.at[d], z_s.at[d], z_r.at[d], ring(-d)) for d in ORDER}
    for d in ORDER:
        gz[d].start()

    dqsum = dqs[0].astype(F32)
    for d in range(1, 8):
        rc(dqs.at[d], dqr.at[d], dq_s.at[d], dq_r.at[d], owner_of(d)).wait_recv()
        dqsum = dqsum + dqr[d].astype(F32)
    dqsum = (dqsum * INV).astype(BF)
    dqf[:, 0:128] = dqsum[0:128]
    dqf[:, 128:256] = dqsum[128:256]
    gx = [
        rc(dqf, dqx.at[i], x_s.at[i], x_r.at[i], dev)
        for i, dev in enumerate((mate, far, far_mate))
    ]
    for cp in (gx[2], gx[1], gx[0]):
        cp.start()

    ksum = zs[0].astype(F32)
    for d in range(1, 8):
        gz[d].wait_recv()
        ksum = ksum + zr[d].astype(F32)
    hs[...] = ksum.astype(BF)
    gh = [
        rc(hs, hr.at[i], h_s.at[i], h_r.at[i], dev)
        for i, dev in enumerate((mate, far, far_mate))
    ]
    for cp in gh:
        cp.start()
    for cp in wpush:
        cp.wait_recv()
    for cp in own[4:]:
        cp.wait()
    for cp in gx:
        cp.wait_recv()
    all_dq = jnp.concatenate([dqf[...], dqx[0], dqx[1], dqx[2]], axis=1)

    def query_part(f, shifts):
        for shift in shifts:
            acc[:, sub(f, shift)] = mm(all_dq, W[:, sub(f, shift)])

    for cp in near[0][2:]:
        cp.wait_recv()
    query_part(0, (0, 1, 2, 4, 6, 7))
    for cp in near[1][:2] + near[1][4:]:
        cp.wait_recv()
    query_part(1, (0, 1, 2, 4, 6, 7))
    for f in range(2):
        for cp in next_near[f]:
            cp.wait_recv()
        query_part(f, (3, 5))

    for cp in gh:
        cp.wait_recv()
    mine = hs[...].astype(F32) + hr[1].astype(F32)
    others = hr[0].astype(F32) + hr[2].astype(F32)
    dk_all = (jnp.where(first_core, mine, others) * INV).astype(BF)
    dv_all = jnp.where(first_core, others, mine).astype(BF)
    kvg = jnp.concatenate([dk_all, dv_all], axis=1)

    def finish(n, carry):
        col = pl.ds(pl.multiple_of(n * 512, 512), 512)
        out[:, col] = (acc[:, col] + mm(kvg, WK[:, col])).astype(BF)
        return carry

    lax.fori_loop(0, 8, finish, 0, unroll=2)

    for d in ORDER:
        for g in (gk, gkv, gmk, gmq, gs[0], gs[1], gz):
            g[d].wait_send()
        for cp in gq[d]:
            cp.wait_send()
        rc(dqs.at[d], dqr.at[d], dq_s.at[d], dq_r.at[d], owner_of(d)).wait_send()
    for cp in wpush + gx + gh + [pair, gk[0]]:
        cp.wait_send()
    for cp in over[0] + over[1] + near[0] + near[1] + next_near[0] + next_near[1]:
        cp.wait_send()


def on_device(queries, keys, values, dout, positions, doc_ids, w_query, w_kv):
    anys = pl.BlockSpec(memory_space=pl.ANY)
    smem = pl.BlockSpec(memory_space=pltpu.SMEM)
    V = pltpu.VMEM
    dma = pltpu.SemaphoreType.DMA
    scratch = [
        V((8, 2, 128, 256), BF), V((2, 8, 128, 128), BF), V((1024, 128), BF),
        V((128, 1024), BF), V((8, 8, 128), F32), V((8, 8, 128), F32), V((8, 128), F32),
        V((128, 256), F32), V((8, 1024, 256), F32), V((8, 1024, 256), F32),
        V((2, 8, 256), F32), V((2, 4, 256), F32), V((8, 2, 8, 256), F32), V((2, 8, 256), F32),
        V((1024, 128), F32), V((1024, 128), F32), V((8, 256, 128), BF), V((8, 256, 128), BF),
        V((1024, 128), BF), V((1024, 128), BF), V((8, 128, 128), BF), V((8, 128, 128), BF),
        V((128, 128), BF), V((3, 128, 128), BF), V((128, 256), BF), V((3, 128, 256), BF),
        V((1024, 4096), BF), V((256, 4096), BF), V((128, 4096), F32),
    ]
    scratch += [dma((8,))] * 12 + [dma((8, 2))] * 2 + [dma((8,))] * 4
    scratch += [dma, dma, dma((3,)), dma((3,)), dma((3,)), dma((3,)), dma, dma]
    scratch += [dma((2, 2)), dma((2, 2)), dma((2, 9)), dma((2, 9)), dma((6,))]
    return pl.pallas_call(
        kernel,
        out_shape=pltpu.VMEM((128, 4096), BF),
        in_specs=[smem, smem] + [anys] * 6,
        out_specs=pl.BlockSpec(memory_space=pltpu.VMEM),
        scratch_shapes=scratch,
        compiler_params=pltpu.CompilerParams(
            collective_id=0, has_side_effects=True, vmem_limit_bytes=60 * 1024 * 1024
        ),
    )(positions, doc_ids, queries, dout, keys, values, w_query, w_kv)


def solution(mesh):
    torus = Mesh(mesh.devices.reshape(8, 2, 4, 2, 2), CTX + HEAD)
    return jax.shard_map(
        on_device,
        mesh=torus,
        in_specs=(
            P(CTX, HEAD),
            P(CTX, None),
            P(CTX, None),
            P(CTX, HEAD),
            P(CTX),
            P(CTX),
            P(HEAD, None),
            P(None, HEAD),
        ),
        out_specs=P(CTX, HEAD),
        check_vma=False,
    )
```
